128 devices in a mesh: sy: 16 (over x_lo, y, core), sx: 8 (over x_hi, z).
Axes of the slice: x: 4 (x_hi: 2, x_lo: 2; x = x_hi * 2 + x_lo), y: 4, z: 4, core: 2. Of those that a mesh axis runs over, the one named last changes fastest.
Arguments:
- spectrum: bfloat16 [2, 18432, 18432], P(None, 'sy', 'sx'), may hold values from -6 to 6
- pupils: bfloat16 [2, 4096, 4096], P(None, 'sy', 'sx'), may hold values from -6 to 6
- amplitudes: float32 [16, 16, 4, 256, 256], P('sy', 'sx'), may hold values from 0.2 to 2
- crop_starts: int32 [16, 16, 4, 2], P('sy', 'sx'), may hold values from 0 to 896
- led_counts: int32 [16, 16], P('sy', 'sx'), may hold values from 1 to 4, as said below
Outputs:
- spectrum_grad: bfloat16 [2, 18432, 18432], P(None, 'sy', 'sx')
- pupil_grad: float32 [2, 4096, 4096], P(None, 'sy', 'sx')
The draws below stay inside these ranges and needn't reach their ends.
Inputs may be any that keep to these rules, and one draw needn't show every extreme that they name: `led_counts`: slots at or past a segment's count are ignored.
All inputs are finite; a program needn't handle non-finite values.
Results may differ from the reference program's by a relative error of at most 0.001.
Values may be sent and summed in bfloat16 or wider, within the bound.
No kernel may reach another device: no remote copies, remote signals or barrier semaphores. Data moves between devices by JAX's collectives and lax.ppermute only.
A program may use at most 256 MiB of HBM per device.

```python
import math
import jax
import jax.numpy as jnp
from jax import lax

W = 256
H = 64
SEG = 1024
MAXL = 4
E = 1152
GY = 16
GX = 16


def draw_crop_starts(key, part):
    subkeys = jax.random.split(key, 2)
    farthest = E - W
    entries = GY * GX * MAXL * 2
    starts = jax.random.randint(subkeys[0], (entries,), 0, farthest + 1)
    chosen = jax.random.permutation(subkeys[1], entries)
    starts = starts.at[chosen[0]].set(0).at[chosen[1]].set(farthest)
    return starts.reshape(GY, GX, MAXL, 2).astype(jnp.int32)


def draw_led_counts(key, part):
    subkeys = jax.random.split(key, 5)
    first_draw = jax.random.randint(subkeys[0], (GY, GX), 1, MAXL + 1)
    second_draw = jax.random.randint(subkeys[1], (GY, GX), 1, MAXL + 1)
    third_draw = jax.random.randint(subkeys[2], (GY, GX), 1, MAXL + 1)
    fewest = jnp.minimum(jnp.minimum(first_draw, second_draw), third_draw)
    pick_row = jax.random.randint(subkeys[3], (), 0, GY)
    pick_col = jax.random.randint(subkeys[4], (), 0, GX // 2) * 2
    fewest = fewest.at[pick_row, pick_col].set(MAXL).at[pick_row, pick_col + 1].set(MAXL)
    return fewest.astype(jnp.int32)


def shard_levels(stream_key, dims, shards, least, top_value):
    def one(dim, parts):
        draws = jax.random.uniform(jax.random.fold_in(jax.random.fold_in(stream_key, 6), dim), (parts,), jnp.float32, least / len(shards), top_value / len(shards))
        return jnp.repeat(jnp.exp(draws), dims[dim] // parts).reshape((-1,) + (1,) * (len(dims) - dim - 1))

    loudness = one(*shards[0])
    for cut in shards[1:]:
        loudness = loudness * one(*cut)
    return loudness


def noise(stream_key, extent, spread, reach, shards=(), kind=jnp.bfloat16):
    level = shard_levels(stream_key, extent, shards, -0.22, 0.18) if shards else 1.0
    values = jax.random.normal(stream_key, extent, jnp.float32) * spread * level
    return jnp.minimum(jnp.maximum(values, -reach), reach).astype(kind)


def setup_inputs(seed: int = 0) -> dict:
    keys = jax.random.split(jax.random.key(seed), 6)
    spectrum = noise(keys[0], (2, GY * E, GX * E), 1.0, 6.0, ((1, 16), (2, 8)))
    pupils = noise(keys[1], (2, GY * W, GX * W), 1.0, 6.0, ((1, 16), (2, 8)))
    amplitudes = jnp.clip(0.2 + 1.8 * jax.random.uniform(keys[2], (GY, GX, MAXL, W, W), jnp.float32) ** shard_levels(keys[2], (GY, GX, MAXL, W, W), ((0, 16), (1, 8)), -0.2, 0.2), 0.2, 2.0)
    crop_starts = draw_crop_starts(jax.random.fold_in(keys[5], 71), 0)
    led_counts = draw_led_counts(jax.random.fold_in(keys[5], 71), 0)
    return dict(spectrum=spectrum, pupils=pupils, amplitudes=amplitudes, crop_starts=crop_starts, led_counts=led_counts)


FLOOR_SQUARE = 0.0625
MU_WEIGHT = 0.5
LAM_WEIGHT = 0.5

def product(first_op, second_op):
    return jnp.dot(first_op, second_op, precision=lax.Precision.HIGHEST, preferred_element_type=jnp.float32)

def dft_tables(side_len):
    positions = jnp.arange(side_len, dtype=jnp.int32)
    phase_index = positions[:, None] * positions[None, :] % side_len
    angles = phase_index.astype(jnp.float32) * (2.0 * math.pi / side_len)
    norm_scale = 1.0 / math.sqrt(side_len)
    return (jnp.cos(angles) * norm_scale, jnp.sin(angles) * norm_scale)

def transform(field_re, field_im, cos_table, sin_table, sign_flip):
    left_re = product(cos_table, field_re) - sign_flip * product(sin_table, field_im)
    left_im = product(cos_table, field_im) + sign_flip * product(sin_table, field_re)
    out_re = product(left_re, cos_table) - sign_flip * product(left_im, sin_table)
    out_im = product(left_im, cos_table) + sign_flip * product(left_re, sin_table)
    return (out_re, out_im)

def segment_data(tile_obj, tile_pup, amp_stack, start_stack, live_count, cos_table, sin_table):
    side_len = tile_pup.shape[1]
    pup_re = tile_pup[0]
    pup_im = tile_pup[1]

    def led_step(slot_index, carried):
        grad_re, grad_im, pgrad_re, pgrad_im = carried
        row_start = start_stack[slot_index, 0]
        col_start = start_stack[slot_index, 1]
        crop_re = lax.dynamic_slice(tile_obj[0], (row_start, col_start), (side_len, side_len))
        crop_im = lax.dynamic_slice(tile_obj[1], (row_start, col_start), (side_len, side_len))
        amp_tile = lax.dynamic_index_in_dim(amp_stack, slot_index, 0, keepdims=False)
        field_re = pup_re * crop_re - pup_im * crop_im
        field_im = pup_re * crop_im + pup_im * crop_re
        psi_re, psi_im = transform(field_re, field_im, cos_table, sin_table, 1.0)
        power_sq = psi_re * psi_re + psi_im * psi_im
        keeper = 1.0 - amp_tile / jnp.sqrt(jnp.maximum(power_sq, FLOOR_SQUARE))
        back_re, back_im = transform(psi_re * keeper, psi_im * keeper, cos_table, sin_table, -1.0)
        dcrop_re = pup_re * back_re + pup_im * back_im
        dcrop_im = pup_re * back_im - pup_im * back_re
        old_re = lax.dynamic_slice(grad_re, (row_start, col_start), (side_len, side_len))
        old_im = lax.dynamic_slice(grad_im, (row_start, col_start), (side_len, side_len))
        grad_re = lax.dynamic_update_slice(grad_re, old_re + dcrop_re, (row_start, col_start))
        grad_im = lax.dynamic_update_slice(grad_im, old_im + dcrop_im, (row_start, col_start))
        pgrad_re = pgrad_re + crop_re * back_re + crop_im * back_im
        pgrad_im = pgrad_im + crop_re * back_im - crop_im * back_re
        return (grad_re, grad_im, pgrad_re, pgrad_im)
    zero_obj = jnp.zeros(tile_obj.shape[1:], jnp.float32)
    zero_pup = jnp.zeros((side_len, side_len), jnp.float32)
    grad_re, grad_im, pgrad_re, pgrad_im = lax.fori_loop(0, live_count, led_step, (zero_obj, zero_obj, zero_pup, zero_pup))
    return (jnp.stack([grad_re, grad_im]), jnp.stack([pgrad_re, pgrad_im]))

def band_range(offset, tile_edge, band_width):
    if offset == 0:
        return (0, 0, tile_edge)
    if offset == 1:
        return (tile_edge - band_width, 0, band_width)
    return (0, tile_edge - band_width, band_width)

def inside(value, limit):
    return jnp.where((value >= 0) & (value < limit), jnp.float32(1.0), jnp.float32(0.0))

def to_tiles(array, grid_rows, grid_cols, tile_edge):
    shaped = array.reshape(2, grid_rows, tile_edge, grid_cols, tile_edge)
    return shaped.transpose(1, 3, 0, 2, 4).reshape(grid_rows * grid_cols, 2, tile_edge, tile_edge)

def from_tiles(tiles, grid_rows, grid_cols, tile_edge):
    shaped = tiles.reshape(grid_rows, grid_cols, 2, tile_edge, tile_edge)
    return shaped.transpose(2, 0, 3, 1, 4).reshape(2, grid_rows * tile_edge, grid_cols * tile_edge)

def reference(spectrum, pupils, amplitudes, crop_starts, led_counts):
    tile_edge = SEG + 2 * H
    band_width = 2 * H
    obj_tiles = to_tiles(spectrum, GY, GX, tile_edge)
    pup_tiles = to_tiles(pupils, GY, GX, W)
    amp_tiles = amplitudes.reshape(GY * GX, MAXL, W, W)
    start_tiles = crop_starts.reshape(GY * GX, MAXL, 2)
    count_tiles = led_counts.reshape(GY * GX)
    cos_table, sin_table = dft_tables(W)

    def one_segment(seg_index):
        seg_row = seg_index // GX
        seg_col = seg_index % GX
        tile_obj = obj_tiles[seg_index].astype(jnp.float32)
        tile_pup = pup_tiles[seg_index].astype(jnp.float32)
        data_obj, data_pup = segment_data(tile_obj, tile_pup, amp_tiles[seg_index], start_tiles[seg_index], count_tiles[seg_index], cos_table, sin_table)
        consist = jnp.zeros_like(tile_obj)
        smooth = jnp.zeros_like(tile_pup)
        for delta_y in (-1, 0, 1):
            for delta_x in (-1, 0, 1):
                if delta_y != 0 or delta_x != 0:
                    near_row = seg_row + delta_y
                    near_col = seg_col + delta_x
                    weight = inside(near_row, GY) * inside(near_col, GX)
                    near_index = jnp.clip(near_row, 0, GY - 1) * GX + jnp.clip(near_col, 0, GX - 1)
                    mine_y, other_y, span_y = band_range(delta_y, tile_edge, band_width)
                    mine_x, other_x, span_x = band_range(delta_x, tile_edge, band_width)
                    neighbour = obj_tiles[near_index][:, other_y:other_y + span_y, other_x:other_x + span_x].astype(jnp.float32)
                    own_band = tile_obj[:, mine_y:mine_y + span_y, mine_x:mine_x + span_x]
                    consist = consist.at[:, mine_y:mine_y + span_y, mine_x:mine_x + span_x].add(weight * (own_band - neighbour))
                    if delta_y == 0 or delta_x == 0:
                        smooth = smooth + weight * (tile_pup - pup_tiles[near_index].astype(jnp.float32))
        grad_obj = (data_obj + MU_WEIGHT * consist).astype(jnp.bfloat16)
        grad_pup = data_pup + LAM_WEIGHT * smooth
        return (grad_obj, grad_pup)
    obj_out, pup_out = lax.map(one_segment, jnp.arange(GY * GX, dtype=jnp.int32))
    return (from_tiles(obj_out, GY, GX, tile_edge), from_tiles(pup_out, GY, GX, W))
```

```python
import functools
import math

import jax
import jax.numpy as jnp
import ml_dtypes
import numpy as np
from jax import lax
from jax.experimental import pallas as pl
from jax.experimental.pallas import tpu as pltpu
from jax.sharding import PartitionSpec as P

H = 64
MAXL = 4
W = 256
HALF = 128
FLOOR_SQUARE = 0.0625
BAND = 2 * H
BF = jnp.bfloat16
F32 = jnp.float32


def halves(table):
    high = table.astype(ml_dtypes.bfloat16)
    low = (table - high.astype(np.float64)).astype(ml_dtypes.bfloat16)
    return high, low


def tables():
    m = np.arange(HALF)[:, None]
    j = np.arange(HALF)[None, :]
    out = []
    for parity in (0, 1):
        phase = ((2 * m + parity) * j % W) * (2.0 * math.pi / W)
        re = np.cos(phase) / math.sqrt(W)
        im = np.sin(phase) / math.sqrt(W)
        left = np.block([[re, -im], [im, re]])
        out.append(left)
        out.append(left.T)
    packed = np.stack([np.stack(halves(t)) for t in out])
    spread = np.zeros((W, W))
    for p in (0, 1):
        for q in range(HALF):
            spread[2 * q + p, p * HALF + q] = 1.0
    return packed, spread.astype(ml_dtypes.bfloat16)


def split(value):
    high = value.astype(BF)
    low = (value - high.astype(F32)).astype(BF)
    return high, low


def dot(a, b):
    return jnp.dot(a, b, preferred_element_type=F32)


def compute_kernel(
    starts, counts, weights, spec_hbm, pup_hbm, amp_hbm, tab_hbm, spread_hbm,
    out_hbm, prow_hbm, pcol_hbm, ppup_hbm,
    spec, pupb, pup, amp, tab, spread, acc, pacc, inner,
    win, prs, xh, xl, ya, yb, ampq, sem_in, sem_out,
):
    edge = spec.shape[2]
    tiles = edge // 128
    low_row, high_row = BAND, edge - BAND
    mid = high_row - low_row
    copies = []
    for g in range(2):
        copies.append(pltpu.make_async_copy(spec_hbm.at[:, :, pl.ds(g * edge, edge)], spec.at[g], sem_in.at[g]))
    copies.append(pltpu.make_async_copy(pup_hbm, pupb, sem_in.at[2]))
    copies.append(pltpu.make_async_copy(tab_hbm, tab, sem_in.at[3]))
    copies.append(pltpu.make_async_copy(spread_hbm, spread, sem_in.at[4]))
    for h in range(2):
        copies.append(pltpu.make_async_copy(amp_hbm.at[0, :, :, :, pl.ds(h * 128, 128)], amp.at[:, :, h], sem_in.at[5 + h]))
    for c in copies:
        c.start()

    zero = jnp.zeros((128, 128), F32)

    def clear(i, carry):
        for g in range(2):
            for c in range(2):
                for k in range(tiles):
                    acc[g, c, k, pl.ds(pl.multiple_of(i * 32, 32), 32), :] = zero[:32]
        return carry

    lax.fori_loop(0, edge // 32, clear, 0)
    for c in copies[2:]:
        c.wait()
    for g in range(2):
        for c in range(2):
            pup[g, c] = pupb[c, :, pl.ds(g * W, W)].astype(F32)
            pacc[g, c] = jnp.zeros((W, W), F32)
    copies[0].wait()
    copies[1].wait()
    lane = lax.broadcasted_iota(jnp.int32, (16, 128), 1)

    def slot_step(g, slot):
        a = starts[(g * MAXL + slot) * 2]
        b = starts[(g * MAXL + slot) * 2 + 1]
        a0 = pl.multiple_of(jnp.minimum(a // 16 * 16, edge - W - 16), 16)
        off = a - a0
        k0 = jnp.minimum(b // 128, tiles - 3)
        s = b - k0 * 128
        sr = lax.rem(s, 128)
        back_shift = lax.rem(128 - sr, 128)
        from_first = lane >= s
        keep_low = lane < 128 - s
        col0 = pl.multiple_of(k0 * 128, 128)
        for c in range(2):
            for r in range(0, W + 16, 16):
                block = spec[g, c, pl.ds(a0 + r, 16), pl.ds(col0, 384)].astype(F32)
                for i in range(3):
                    win[c, i, pl.ds(r, 16), :] = block[:, i * 128 : (i + 1) * 128]
        for c in range(2):
            for r in range(0, W, 16):
                r0 = pltpu.roll(pup[g, c, pl.ds(r, 16), pl.ds(0, 128)], sr, 1)
                r1 = pltpu.roll(pup[g, c, pl.ds(r, 16), pl.ds(128, 128)], sr, 1)
                prs[c, 0, pl.ds(r, 16), :] = jnp.where(from_first, r0, r1)
                prs[c, 1, pl.ds(r, 16), :] = jnp.where(from_first, r1, r0)

        def crop(c, h, r):
            if h == 1:
                return win[c, 1, pl.ds(off + r, 16), :]
            return jnp.where(from_first, win[c, 0, pl.ds(off + r, 16), :], win[c, 2, pl.ds(off + r, 16), :])

        for p in range(2):
            for h in range(2):
                rows = amp[g, slot, h, pl.ds(p, 128, stride=2), :]
                hi, lo = split(rows)
                xh[0, pl.ds(p * 128, 128), pl.ds(h * 128, 128)] = hi
                xl[0, pl.ds(p * 128, 128), pl.ds(h * 128, 128)] = lo
        ampq[...] = dot(xh[0], spread[...]) + dot(xl[0], spread[...])

        for r in range(0, HALF, 16):
            for h in range(2):
                parts = []
                for rr in (r, r + HALF):
                    cr = crop(0, h, rr)
                    ci = crop(1, h, rr)
                    pr = prs[0, h, pl.ds(rr, 16), :]
                    pi = prs[1, h, pl.ds(rr, 16), :]
                    parts.append((pr * cr - pi * ci, pr * ci + pi * cr))
                for c in range(2):
                    for q in range(2):
                        v = parts[0][c] + parts[1][c] if q == 0 else parts[0][c] - parts[1][c]
                        hi, lo = split(v)
                        xh[q, pl.ds(c * HALF + r, 16), pl.ds(h * 128, 128)] = hi
                        xl[q, pl.ds(c * HALF + r, 16), pl.ds(h * 128, 128)] = lo
        for q in range(2):
            th, tl = tab[2 * q, 0], tab[2 * q, 1]
            ya[q] = dot(th, xh[q]) + dot(th, xl[q]) + dot(tl, xh[q])
        for q in range(2):
            for r in range(0, HALF, 16):
                for c in range(2):
                    y0 = ya[q, pl.ds(c * HALF + r, 16), pl.ds(0, 128)]
                    y1 = ya[q, pl.ds(c * HALF + r, 16), pl.ds(128, 128)]
                    for u in range(2):
                        hi, lo = split(y0 + y1 if u == 0 else y0 - y1)
                        xh[u, pl.ds(q * HALF + r, 16), pl.ds(c * 128, 128)] = hi
                        xl[u, pl.ds(q * HALF + r, 16), pl.ds(c * 128, 128)] = lo
        for u in range(2):
            th, tl = tab[2 * u + 1, 0], tab[2 * u + 1, 1]
            yb[u] = dot(xh[u], th) + dot(xl[u], th) + dot(xh[u], tl)
        for u in range(2):
            for r in range(0, W, 16):
                re = yb[u, pl.ds(r, 16), pl.ds(0, 128)]
                im = yb[u, pl.ds(r, 16), pl.ds(128, 128)]
                power = jnp.maximum(re * re + im * im, FLOOR_SQUARE)
                keeper = 1.0 - ampq[pl.ds(r, 16), pl.ds(u * 128, 128)] * lax.rsqrt(power)
                for c, v in enumerate((re, im)):
                    hi, lo = split(v * keeper)
                    xh[u, pl.ds(r, 16), pl.ds(c * 128, 128)] = hi
                    xl[u, pl.ds(r, 16), pl.ds(c * 128, 128)] = lo
        for u in range(2):
            th, tl = tab[2 * u, 0], tab[2 * u, 1]
            ya[u] = dot(xh[u], th) + dot(xl[u], th) + dot(xh[u], tl)
        for q in range(2):
            for r in range(0, HALF, 16):
                for c in range(2):
                    e = ya[0, pl.ds(q * HALF + r, 16), pl.ds(c * 128, 128)]
                    o = ya[1, pl.ds(q * HALF + r, 16), pl.ds(c * 128, 128)]
                    for h in range(2):
                        hi, lo = split(e + o if h == 0 else e - o)
                        xh[q, pl.ds(c * HALF + r, 16), pl.ds(h * 128, 128)] = hi
                        xl[q, pl.ds(c * HALF + r, 16), pl.ds(h * 128, 128)] = lo
        for q in range(2):
            th, tl = tab[2 * q + 1, 0], tab[2 * q + 1, 1]
            yb[q] = dot(th, xh[q]) + dot(th, xl[q]) + dot(tl, xh[q])
        for r in range(0, HALF, 16):
            for rr in (r, r + HALF):
                back = []
                for c in range(2):
                    row = []
                    for h in range(2):
                        e = yb[0, pl.ds(c * HALF + r, 16), pl.ds(h * 128, 128)]
                        o = yb[1, pl.ds(c * HALF + r, 16), pl.ds(h * 128, 128)]
                        row.append(e + o if rr == r else e - o)
                    back.append(row)
                terms = []
                for h in range(2):
                    br, bi = back[0][h], back[1][h]
                    pr = prs[0, h, pl.ds(rr, 16), :]
                    pi = prs[1, h, pl.ds(rr, 16), :]
                    cr = crop(0, h, rr)
                    ci = crop(1, h, rr)
                    drop = (pr * br + pi * bi, pr * bi - pi * br)
                    terms.append((cr * br + ci * bi, cr * bi - ci * br))
                    rows = pl.ds(a + rr, 16)
                    for c in range(2):
                        if h == 1:
                            acc[g, c, k0 + 1, rows, :] += drop[c]
                        else:
                            acc[g, c, k0, rows, :] += jnp.where(from_first, drop[c], 0.0)
                            acc[g, c, k0 + 2, rows, :] += jnp.where(from_first, 0.0, drop[c])
                for c in range(2):
                    t0 = pltpu.roll(terms[0][c], back_shift, 1)
                    t1 = pltpu.roll(terms[1][c], back_shift, 1)
                    pacc[g, c, pl.ds(rr, 16), pl.ds(0, 128)] += jnp.where(keep_low, t0, t1)
                    pacc[g, c, pl.ds(rr, 16), pl.ds(128, 128)] += jnp.where(keep_low, t1, t0)

    up, down, left_out, right_out = weights[0], weights[1], weights[2], weights[3]
    pending = []

    def put(src, dst):
        copy = pltpu.make_async_copy(src, dst, sem_out.at[len(pending)])
        copy.start()
        pending.append(copy)

    for g in range(2):

        def step(slot, carry, g=g):
            slot_step(g, slot)
            return carry

        lax.fori_loop(0, counts[g], step, 0)
        left = left_out if g == 0 else F32(1.0)
        right = right_out if g == 1 else F32(1.0)
        neighbours = up + down + left + right
        for c in range(2):
            pacc[g, c] = pacc[g, c] + 0.5 * (neighbours * pup[g, c] - pup[1 - g, c])
            put(pacc.at[g, c], ppup_hbm.at[c, :, pl.ds(g * W, W)])
        for c in range(2):
            for k in range(tiles):
                side = left if k == 0 else right if k == tiles - 1 else None
                local = (k == 0 and g == 1) or (k == tiles - 1 and g == 0)
                for t, (first, vert) in enumerate(((0, up), (high_row, down))):
                    factor = vert if side is None else (1.0 + vert) * (1.0 + side) - 1.0
                    own = spec[g, c, pl.ds(first, BAND), pl.ds(k * 128, 128)].astype(F32)
                    add = (0.5 * factor) * own
                    if local:
                        other = spec[1 - g, c, pl.ds(first, BAND), pl.ds((tiles - 1 - k) * 128, 128)].astype(F32)
                        add = add - 0.5 * other
                    acc[g, c, k, pl.ds(first, BAND), :] += add
            for t, first in enumerate((0, high_row)):
                put(acc.at[g, c, :, pl.ds(first, BAND), :], prow_hbm.at[t, c, pl.ds(g * tiles, tiles)])
        k_out = 0 if g == 0 else tiles - 1
        w_out = left_out if g == 0 else right_out
        for c in range(2):

            def outer(i, carry, c=c):
                rows = pl.ds(pl.multiple_of(low_row + i * 128, 128), 128)
                acc[g, c, k_out, rows, :] += (0.5 * w_out) * spec[g, c, rows, pl.ds(k_out * 128, 128)].astype(F32)
                return carry

            lax.fori_loop(0, mid // 128, outer, 0)
            put(acc.at[g, c, k_out, pl.ds(low_row, mid), :], pcol_hbm.at[g, c])
        k_in = tiles - 1 if g == 0 else 0
        first_tile = 1 if g == 0 else 0
        for c in range(2):

            def finish(i, carry, c=c):
                rows = pl.ds(pl.multiple_of(low_row + i * 64, 64), 64)
                dst = pl.ds(pl.multiple_of(i * 64, 64), 64)
                for k in range(first_tile, first_tile + tiles - 1):
                    v = acc[g, c, k, rows, :]
                    if k == k_in:
                        own = spec[g, c, rows, pl.ds(k * 128, 128)].astype(F32)
                        other = spec[1 - g, c, rows, pl.ds((tiles - 1 - k) * 128, 128)].astype(F32)
                        v = v + 0.5 * (own - other)
                    inner[g, c, dst, pl.ds((k - first_tile) * 128, 128)] = v.astype(BF)
                return carry

            lax.fori_loop(0, mid // 64, finish, 0)
            put(
                inner.at[g, c],
                out_hbm.at[c, pl.ds(low_row, mid), pl.ds((g * tiles + first_tile) * 128, (tiles - 1) * 128)],
            )
    for copy in pending:
        copy.wait()


def compute(spectrum, pupils, amplitudes, starts, counts, weights):
    edge = spectrum.shape[1]
    tiles = edge // 128
    mid = edge - 2 * BAND
    packed, spread = tables()
    hbm = pl.BlockSpec(memory_space=pl.ANY)
    smem = pl.BlockSpec(memory_space=pltpu.SMEM)
    return pl.pallas_call(
        compute_kernel,
        out_shape=(
            jax.ShapeDtypeStruct(spectrum.shape, BF),
            jax.ShapeDtypeStruct((2, 2, 2 * tiles, BAND, 128), F32),
            jax.ShapeDtypeStruct((2, 2, mid, 128), F32),
            jax.ShapeDtypeStruct(pupils.shape, F32),
        ),
        in_specs=[smem, smem, smem, hbm, hbm, hbm, hbm, hbm],
        out_specs=(hbm, hbm, hbm, hbm),
        scratch_shapes=[
            pltpu.VMEM((2, 2, edge, edge), BF),
            pltpu.VMEM((2, W, 2 * W), BF),
            pltpu.VMEM((2, 2, W, W), F32),
            pltpu.VMEM((2, MAXL, 2, W, 128), F32),
            pltpu.VMEM((4, 2, W, W), BF),
            pltpu.VMEM((W, W), BF),
            pltpu.VMEM((2, 2, tiles, edge, 128), F32),
            pltpu.VMEM((2, 2, W, W), F32),
            pltpu.VMEM((2, 2, mid, (tiles - 1) * 128), BF),
            pltpu.VMEM((2, 3, W + 16, 128), F32),
            pltpu.VMEM((2, 2, W, 128), F32),
            pltpu.VMEM((2, W, W), BF),
            pltpu.VMEM((2, W, W), BF),
            pltpu.VMEM((2, W, W), F32),
            pltpu.VMEM((2, W, W), F32),
            pltpu.VMEM((W, W), F32),
            pltpu.SemaphoreType.DMA((7,)),
            pltpu.SemaphoreType.DMA((20,)),
        ],
        compiler_params=pltpu.CompilerParams(vmem_limit_bytes=52 * 1024 * 1024),
        cost_estimate=pl.CostEstimate(flops=20_000_000_000, bytes_accessed=30_000_000, transcendentals=0),
        name="data_terms",
    )(starts, counts, weights, spectrum, pupils, amplitudes, jnp.asarray(packed), jnp.asarray(spread))


def finish_kernel(
    out_in, prow_hbm, pcol_hbm, ppup_hbm, up_hbm, down_hbm, left_hbm, right_hbm, ul_hbm, ur_hbm, dl_hbm, dr_hbm,
    out_hbm, pup_hbm,
    prow, pcol, ppup, vert, side, diag, rows_out, cols_out, pup_out, sem_in, sem_out,
):
    edge = out_in.shape[1]
    tiles = edge // 128
    mid = edge - 2 * BAND
    high_row = edge - BAND
    last = 2 * tiles - 1
    ins = {}

    def get(name, src, dst):
        copy = pltpu.make_async_copy(src, dst, sem_in.at[len(ins)])
        copy.start()
        ins[name] = copy

    verts = (up_hbm, down_hbm)
    sides = (left_hbm, right_hbm)
    diags = ((ul_hbm, ur_hbm), (dl_hbm, dr_hbm))
    for d in range(2):
        get(("side", d), sides[d], side.at[d])
    for t in range(2):
        get(("vert", t), verts[t], vert.at[t])
        for d in range(2):
            get(("diag", t, d), diags[t][d], diag.at[t, d])
        get(("prow", t), prow_hbm.at[t], prow.at[t])
    for d in range(2):
        get(("pcol", d), pcol_hbm.at[d], pcol.at[d])
    get("ppup", ppup_hbm, ppup)
    outs = []

    def put(src, dst):
        copy = pltpu.make_async_copy(src, dst, sem_out.at[len(outs)])
        copy.start()
        outs.append(copy)

    ins["side", 0].wait()
    ins["side", 1].wait()
    for t in range(2):
        ins["vert", t].wait()
        ins["diag", t, 0].wait()
        ins["diag", t, 1].wait()
        ins["prow", t].wait()
        first = t * high_row
        for c in range(2):
            for k in range(2 * tiles):
                sub = vert[t, c, :, pl.ds(k * 128, 128)].astype(F32)
                if k == tiles - 1 or k == tiles:
                    sub = sub + vert[t, c, :, pl.ds((2 * tiles - 1 - k) * 128, 128)].astype(F32)
                if k == 0 or k == last:
                    d = 0 if k == 0 else 1
                    sub = sub + (diag[t, d, c].astype(F32) + side[d, c, pl.ds(first, BAND), :].astype(F32))
                rows_out[t, c, :, pl.ds(k * 128, 128)] = (prow[t, c, k] - 0.5 * sub).astype(BF)
            put(rows_out.at[t, c], out_hbm.at[c, pl.ds(first, BAND), :])
    for d in range(2):
        ins["pcol", d].wait()
        for c in range(2):
            sub = side[d, c, pl.ds(BAND, mid), :].astype(F32)
            cols_out[d, c] = (pcol[d, c] - 0.5 * sub).astype(BF)
            put(cols_out.at[d, c], out_hbm.at[c, pl.ds(BAND, mid), pl.ds(d * last * 128, 128)])
    ins["ppup"].wait()
    for c in range(2):
        for half in range(2):
            rows = pl.ds(half * 128, 128)
            for q in range(4):
                cols = pl.ds(q * 128, 128)
                d = q // 2
                sub = side[d, c, pl.ds(edge + (q % 2) * W + half * 128, 128), :].astype(F32)
                for t in range(2):
                    sub = sub + vert[t, c, :, pl.ds(2 * edge + half * 512 + q * 128, 128)].astype(F32)
                pup_out[c, rows, cols] = ppup[c, rows, cols] - 0.5 * sub
    put(pup_out, pup_hbm)
    for copy in outs:
        copy.wait()


def finish(out, prow, pcol, ppup, ups, sides, diags):
    edge = out.shape[1]
    tiles = edge // 128
    mid = edge - 2 * BAND
    hbm = pl.BlockSpec(memory_space=pl.ANY)
    return pl.pallas_call(
        finish_kernel,
        out_shape=(
            jax.ShapeDtypeStruct(out.shape, BF),
            jax.ShapeDtypeStruct(ppup.shape, F32),
        ),
        in_specs=[hbm] * 12,
        out_specs=(hbm, hbm),
        input_output_aliases={0: 0},
        scratch_shapes=[
            pltpu.VMEM(prow.shape, F32),
            pltpu.VMEM(pcol.shape, F32),
            pltpu.VMEM(ppup.shape, F32),
            pltpu.VMEM((2,) + ups[0].shape, BF),
            pltpu.VMEM((2,) + sides[0].shape, BF),
            pltpu.VMEM((2, 2) + diags[0].shape, BF),
            pltpu.VMEM((2, 2, BAND, 2 * edge), BF),
            pltpu.VMEM((2, 2, mid, 128), BF),
            pltpu.VMEM(ppup.shape, F32),
            pltpu.SemaphoreType.DMA((16,)),
            pltpu.SemaphoreType.DMA((9,)),
        ],
        compiler_params=pltpu.CompilerParams(vmem_limit_bytes=32 * 1024 * 1024),
        cost_estimate=pl.CostEstimate(flops=10_000_000, bytes_accessed=17_000_000, transcendentals=0),
        name="shared_bands",
    )(out, prow, pcol, ppup, *ups, *sides, *diags)


def local(spectrum, pupils, amplitudes, crop_starts, led_counts):
    edge = spectrum.shape[1]
    wide = spectrum.shape[2]
    rows = lax.axis_size("sy")
    cols = lax.axis_size("sx")
    row = lax.axis_index("sy")
    col = lax.axis_index("sx")

    def chain(count, step):
        return [(i, i + step) for i in range(count) if 0 <= i + step < count]

    def corner(dy, dx):
        return [
            (y * cols + x, (y + dy) * cols + x + dx)
            for y in range(rows)
            for x in range(cols)
            if 0 <= y + dy < rows and 0 <= x + dx < cols
        ]

    def side_pack(first, half):
        band = spectrum[:, :, first : first + BAND]
        tile = pupils[:, :, half * W : (half + 1) * W]
        return jnp.concatenate([band, tile[:, :, :128], tile[:, :, 128:]], axis=1)

    def vert_pack(first):
        band = spectrum[:, first : first + BAND, :]
        return jnp.concatenate([band, pupils[:, :128, :], pupils[:, 128:, :]], axis=2)

    from_left = lax.ppermute(side_pack(wide - BAND, 1), "sx", chain(cols, 1))
    from_right = lax.ppermute(side_pack(0, 0), "sx", chain(cols, -1))
    from_up = lax.ppermute(vert_pack(edge - BAND), "sy", chain(rows, 1))
    from_down = lax.ppermute(vert_pack(0), "sy", chain(rows, -1))
    diags = []
    for dy in (-1, 1):
        for dx in (-1, 1):
            y0 = edge - BAND if dy < 0 else 0
            x0 = wide - BAND if dx < 0 else 0
            piece = spectrum[:, y0 : y0 + BAND, x0 : x0 + BAND]
            diags.append(lax.ppermute(piece, ("sy", "sx"), corner(-dy, -dx)))
    weights = jnp.stack([row > 0, row < rows - 1, col > 0, col < cols - 1]).astype(F32)
    out, prow, pcol, ppup = compute(
        spectrum, pupils, amplitudes, crop_starts.reshape(-1), led_counts.reshape(-1), weights
    )
    return finish(out, prow, pcol, ppup, (from_up, from_down), (from_left, from_right), diags)


def solution(mesh):
    placed = (
        P(None, "sy", "sx"),
        P(None, "sy", "sx"),
        P("sy", "sx", None, None, None),
        P("sy", "sx", None, None),
        P("sy", "sx"),
    )
    return jax.shard_map(
        local,
        mesh=mesh,
        in_specs=placed,
        out_specs=(P(None, "sy", "sx"), P(None, "sy", "sx")),
        check_vma=False,
    )
```

```python
import functools
import math

import jax
import jax.numpy as jnp
import ml_dtypes
import numpy as np
from jax import lax
from jax.experimental import pallas as pl
from jax.experimental.pallas import tpu as pltpu
from jax.sharding import PartitionSpec as P

H = 64
MAXL = 4
W = 256
HALF = 128
FLOOR_SQUARE = 0.0625
PACK_VMEM = 60 * 1024 * 1024
CORNER_VMEM = 8 * 1024 * 1024
FINISH_VMEM = 66500000
BAND = 2 * H
BF = jnp.bfloat16
F32 = jnp.float32


def halves(table):
    high = table.astype(ml_dtypes.bfloat16)
    low = (table - high.astype(np.float64)).astype(ml_dtypes.bfloat16)
    return high, low


def tables():
    m = np.arange(HALF)[:, None]
    j = np.arange(HALF)[None, :]
    out = []
    for parity in (0, 1):
        phase = ((2 * m + parity) * j % W) * (2.0 * math.pi / W)
        re = np.cos(phase) / math.sqrt(W)
        im = np.sin(phase) / math.sqrt(W)
        left = np.block([[re, -im], [im, re]])
        out.append(left)
        out.append(left.T)
    packed = np.stack([np.stack([halves(t)[part] for t in out]) for part in (0, 1)])
    spread = np.zeros((W, W))
    for p in (0, 1):
        for q in range(HALF):
            spread[2 * q + p, p * HALF + q] = 1.0
    spread = np.concatenate([spread, spread]).astype(ml_dtypes.bfloat16)
    return packed, spread


def split(value):
    high = value.astype(BF)
    low = (value - high.astype(F32)).astype(BF)
    return high, low


def dot(a, b):
    return jnp.dot(a, b, preferred_element_type=F32)


def put_rows(ref, index, rows, cols, value):
    high, low = split(value)
    ref[index, pl.ds(rows, 16), cols] = high
    ref[index, pl.ds(W + rows, 16), cols] = low
    ref[index, pl.ds(2 * W + rows, 16), cols] = high


def put_cols(ref, index, rows, cols, value):
    high, low = split(value)
    ref[index, rows, pl.ds(cols, 128)] = high
    ref[index, rows, pl.ds(W + cols, 128)] = low
    ref[index, rows, pl.ds(2 * W + cols, 128)] = high


def compute_kernel(
    starts, counts, weights, spec_hbm, pup_hbm, amp_hbm, tab_hbm, spread_hbm,
    out_hbm, prow_hbm, pcol_hbm, ppup_hbm,
    spec, pupb, pup, amp, tab_l, tab_r, spread, acc, pacc, inner,
    win, prs, xr, xc, xa, ya, yb, ampq, sem_in, sem_out,
):
    edge = spec.shape[2]
    tiles = edge // 128
    low_row, high_row = BAND, edge - BAND
    mid = high_row - low_row
    copies = []

    def get(src, dst):
        copy = pltpu.make_async_copy(src, dst, sem_in.at[len(copies)])
        copy.start()
        copies.append(copy)

    get(pup_hbm, pupb)
    for h in range(2):
        get(amp_hbm.at[0, :, :, :, pl.ds(h * 128, 128)], amp.at[:, :, h])
    for i, part in enumerate((0, 0, 1)):
        get(tab_hbm.at[part], tab_l.at[:, :, pl.ds(i * W, W)])
        get(tab_hbm.at[part], tab_r.at[:, pl.ds(i * W, W), :])
    get(spread_hbm, spread)
    for g in range(2):
        get(spec_hbm.at[:, :, pl.ds(g * edge, edge)], spec.at[g])

    zero = jnp.zeros((128, 128), F32)

    def clear(i, carry):
        for g in range(2):
            for c in range(2):
                for k in range(tiles):
                    acc[g, c, k, pl.ds(pl.multiple_of(i * 32, 32), 32), :] = zero[:32]
        return carry

    lax.fori_loop(0, edge // 32, clear, 0)
    for c in copies[:-2]:
        c.wait()
    for g in range(2):
        for c in range(2):
            pup[g, c] = pupb[c, :, pl.ds(g * W, W)].astype(F32)
            pacc[g, c] = jnp.zeros((W, W), F32)
    copies[-2].wait()
    lane = lax.broadcasted_iota(jnp.int32, (16, 128), 1)

    def slot_step(g, slot):
        a = starts[(g * MAXL + slot) * 2]
        b = starts[(g * MAXL + slot) * 2 + 1]
        a0 = pl.multiple_of(jnp.minimum(a // 16 * 16, edge - W - 16), 16)
        off = a - a0
        k0 = jnp.minimum(b // 128, tiles - 3)
        s = b - k0 * 128
        sr = lax.rem(s, 128)
        back_shift = lax.rem(128 - sr, 128)
        from_first = lane >= s
        keep_low = lane < 128 - s
        col0 = pl.multiple_of(k0 * 128, 128)
        for c in range(2):
            for r in range(0, W + 16, 16):
                block = spec[g, c, pl.ds(a0 + r, 16), pl.ds(col0, 384)].astype(F32)
                for i in range(3):
                    win[c, i, pl.ds(r, 16), :] = block[:, i * 128 : (i + 1) * 128]
        for c in range(2):
            for r in range(0, W, 16):
                r0 = pltpu.roll(pup[g, c, pl.ds(r, 16), pl.ds(0, 128)], sr, 1)
                r1 = pltpu.roll(pup[g, c, pl.ds(r, 16), pl.ds(128, 128)], sr, 1)
                prs[c, 0, pl.ds(r, 16), :] = jnp.where(from_first, r0, r1)
                prs[c, 1, pl.ds(r, 16), :] = jnp.where(from_first, r1, r0)

        def crop(c, h, r):
            if h == 1:
                return win[c, 1, pl.ds(off + r, 16), :]
            return jnp.where(from_first, win[c, 0, pl.ds(off + r, 16), :], win[c, 2, pl.ds(off + r, 16), :])

        for p in range(2):
            for h in range(2):
                rows = amp[g, slot, h, pl.ds(p, 128, stride=2), :]
                hi, lo = split(rows)
                xa[pl.ds(p * 128, 128), pl.ds(h * 128, 128)] = hi
                xa[pl.ds(p * 128, 128), pl.ds(W + h * 128, 128)] = lo
        ampq[...] = dot(xa[...], spread[...])

        for r in range(0, HALF, 16):
            for h in range(2):
                parts = []
                for rr in (r, r + HALF):
                    cr = crop(0, h, rr)
                    ci = crop(1, h, rr)
                    pr = prs[0, h, pl.ds(rr, 16), :]
                    pi = prs[1, h, pl.ds(rr, 16), :]
                    parts.append((pr * cr - pi * ci, pr * ci + pi * cr))
                for c in range(2):
                    cols = pl.ds(h * 128, 128)
                    put_rows(xr, 0, c * HALF + r, cols, parts[0][c] + parts[1][c])
                    put_rows(xr, 1, c * HALF + r, cols, parts[0][c] - parts[1][c])
        for q in range(2):
            ya[q] = dot(tab_l[2 * q], xr[q])
        for q in range(2):
            for r in range(0, HALF, 16):
                rows = pl.ds(q * HALF + r, 16)
                for c in range(2):
                    y0 = ya[q, pl.ds(c * HALF + r, 16), pl.ds(0, 128)]
                    y1 = ya[q, pl.ds(c * HALF + r, 16), pl.ds(128, 128)]
                    put_cols(xc, 0, rows, c * 128, y0 + y1)
                    put_cols(xc, 1, rows, c * 128, y0 - y1)
        for u in range(2):
            yb[u] = dot(xc[u], tab_r[2 * u + 1])
        for u in range(2):
            for r in range(0, W, 16):
                rows = pl.ds(r, 16)
                re = yb[u, rows, pl.ds(0, 128)]
                im = yb[u, rows, pl.ds(128, 128)]
                power = jnp.maximum(re * re + im * im, FLOOR_SQUARE)
                keeper = 1.0 - ampq[rows, pl.ds(u * 128, 128)] * lax.rsqrt(power)
                put_cols(xc, u, rows, 0, re * keeper)
                put_cols(xc, u, rows, 128, im * keeper)
        for u in range(2):
            ya[u] = dot(xc[u], tab_r[2 * u])
        for q in range(2):
            for r in range(0, HALF, 16):
                rows = pl.ds(q * HALF + r, 16)
                for c in range(2):
                    e = ya[0, rows, pl.ds(c * 128, 128)]
                    o = ya[1, rows, pl.ds(c * 128, 128)]
                    put_rows(xr, q, c * HALF + r, pl.ds(0, 128), e + o)
                    put_rows(xr, q, c * HALF + r, pl.ds(128, 128), e - o)
        for q in range(2):
            yb[q] = dot(tab_l[2 * q + 1], xr[q])
        for r in range(0, HALF, 16):
            for rr in (r, r + HALF):
                rows = pl.ds(a + rr, 16)
                old = [[acc[g, c, k0 + i, rows, :] for i in range(3)] for c in range(2)]
                drop, terms = [], []
                for h in range(2):
                    back = []
                    for c in range(2):
                        e = yb[0, pl.ds(c * HALF + r, 16), pl.ds(h * 128, 128)]
                        o = yb[1, pl.ds(c * HALF + r, 16), pl.ds(h * 128, 128)]
                        back.append(e + o if rr == r else e - o)
                    br, bi = back
                    pr = prs[0, h, pl.ds(rr, 16), :]
                    pi = prs[1, h, pl.ds(rr, 16), :]
                    cr = crop(0, h, rr)
                    ci = crop(1, h, rr)
                    drop.append((pr * br + pi * bi, pr * bi - pi * br))
                    terms.append((cr * br + ci * bi, cr * bi - ci * br))
                for c in range(2):
                    acc[g, c, k0, rows, :] = old[c][0] + jnp.where(from_first, drop[0][c], 0.0)
                    acc[g, c, k0 + 1, rows, :] = old[c][1] + drop[1][c]
                    acc[g, c, k0 + 2, rows, :] = old[c][2] + jnp.where(from_first, 0.0, drop[0][c])
                for c in range(2):
                    t0 = pltpu.roll(terms[0][c], back_shift, 1)
                    t1 = pltpu.roll(terms[1][c], back_shift, 1)
                    pacc[g, c, pl.ds(rr, 16), pl.ds(0, 128)] += jnp.where(keep_low, t0, t1)
                    pacc[g, c, pl.ds(rr, 16), pl.ds(128, 128)] += jnp.where(keep_low, t1, t0)

    up, down, left_out, right_out = weights[0], weights[1], weights[2], weights[3]
    pending = []

    def put(src, dst):
        copy = pltpu.make_async_copy(src, dst, sem_out.at[len(pending)])
        copy.start()
        pending.append(copy)

    for g in range(2):

        def step(slot, carry, g=g):
            slot_step(g, slot)
            return carry

        lax.fori_loop(0, counts[g], step, 0)
        if g == 0:
            copies[-1].wait()
        left = left_out if g == 0 else F32(1.0)
        right = right_out if g == 1 else F32(1.0)
        neighbours = up + down + left + right
        for c in range(2):
            pacc[g, c] = pacc[g, c] + 0.5 * (neighbours * pup[g, c] - pup[1 - g, c])
            put(pacc.at[g, c], ppup_hbm.at[c, :, pl.ds(g * W, W)])
        for c in range(2):
            for k in range(tiles):
                side = left if k == 0 else right if k == tiles - 1 else None
                local = (k == 0 and g == 1) or (k == tiles - 1 and g == 0)
                for t, (first, vert) in enumerate(((0, up), (high_row, down))):
                    factor = vert if side is None else (1.0 + vert) * (1.0 + side) - 1.0
                    own = spec[g, c, pl.ds(first, BAND), pl.ds(k * 128, 128)].astype(F32)
                    add = (0.5 * factor) * own
                    if local:
                        other = spec[1 - g, c, pl.ds(first, BAND), pl.ds((tiles - 1 - k) * 128, 128)].astype(F32)
                        add = add - 0.5 * other
                    acc[g, c, k, pl.ds(first, BAND), :] += add
            for t, first in enumerate((0, high_row)):
                put(acc.at[g, c, :, pl.ds(first, BAND), :], prow_hbm.at[t, c, pl.ds(g * tiles, tiles)])
        k_out = 0 if g == 0 else tiles - 1
        w_out = left_out if g == 0 else right_out
        for c in range(2):

            def outer(i, carry, c=c):
                rows = pl.ds(pl.multiple_of(low_row + i * 128, 128), 128)
                acc[g, c, k_out, rows, :] += (0.5 * w_out) * spec[g, c, rows, pl.ds(k_out * 128, 128)].astype(F32)
                return carry

            lax.fori_loop(0, mid // 128, outer, 0)
            put(acc.at[g, c, k_out, pl.ds(low_row, mid), :], pcol_hbm.at[g, c])
        k_in = tiles - 1 if g == 0 else 0
        first_tile = 1 if g == 0 else 0
        for c in range(2):

            def finish(i, carry, c=c):
                rows = pl.ds(pl.multiple_of(low_row + i * 64, 64), 64)
                dst = pl.ds(pl.multiple_of(i * 64, 64), 64)
                for k in range(first_tile, first_tile + tiles - 1):
                    v = acc[g, c, k, rows, :]
                    if k == k_in:
                        own = spec[g, c, rows, pl.ds(k * 128, 128)].astype(F32)
                        other = spec[1 - g, c, rows, pl.ds((tiles - 1 - k) * 128, 128)].astype(F32)
                        v = v + 0.5 * (own - other)
                    inner[g, c, dst, pl.ds((k - first_tile) * 128, 128)] = v.astype(BF)
                return carry

            lax.fori_loop(0, mid // 64, finish, 0)
            put(
                inner.at[g, c],
                out_hbm.at[c, pl.ds(low_row, mid), pl.ds((g * tiles + first_tile) * 128, (tiles - 1) * 128)],
            )
    for copy in pending:
        copy.wait()


def compute(spectrum, pupils, amplitudes, starts, counts, weights):
    edge = spectrum.shape[1]
    tiles = edge // 128
    mid = edge - 2 * BAND
    packed, spread = tables()
    hbm = pl.BlockSpec(memory_space=pl.ANY)
    smem = pl.BlockSpec(memory_space=pltpu.SMEM)
    return pl.pallas_call(
        compute_kernel,
        out_shape=(
            jax.ShapeDtypeStruct(spectrum.shape, BF),
            jax.ShapeDtypeStruct((2, 2, 2 * tiles, BAND, 128), F32),
            jax.ShapeDtypeStruct((2, 2, mid, 128), F32),
            jax.ShapeDtypeStruct(pupils.shape, F32),
        ),
        in_specs=[smem, smem, smem] + [hbm] * 5,
        out_specs=(hbm, hbm, hbm, hbm),
        scratch_shapes=[
            pltpu.VMEM((2, 2, edge, edge), BF),
            pltpu.VMEM((2, W, 2 * W), BF),
            pltpu.VMEM((2, 2, W, W), F32),
            pltpu.VMEM((2, MAXL, 2, W, 128), F32),
            pltpu.VMEM((4, W, 3 * W), BF),
            pltpu.VMEM((4, 3 * W, W), BF),
            pltpu.VMEM((2 * W, W), BF),
            pltpu.VMEM((2, 2, tiles, edge, 128), F32),
            pltpu.VMEM((2, 2, W, W), F32),
            pltpu.VMEM((2, 2, mid, (tiles - 1) * 128), BF),
            pltpu.VMEM((2, 3, W + 16, 128), F32),
            pltpu.VMEM((2, 2, W, 128), F32),
            pltpu.VMEM((2, 3 * W, W), BF),
            pltpu.VMEM((2, W, 3 * W), BF),
            pltpu.VMEM((W, 2 * W), BF),
            pltpu.VMEM((2, W, W), F32),
            pltpu.VMEM((2, W, W), F32),
            pltpu.VMEM((W, W), F32),
            pltpu.SemaphoreType.DMA((12,)),
            pltpu.SemaphoreType.DMA((20,)),
        ],
        compiler_params=pltpu.CompilerParams(vmem_limit_bytes=66500000),
        cost_estimate=pl.CostEstimate(flops=20_000_000_000, bytes_accessed=30_000_000, transcendentals=0),
        name="data_terms",
    )(starts, counts, weights, spectrum, pupils, amplitudes, jnp.asarray(packed), jnp.asarray(spread))


def finish_kernel(
    out_in, prow_hbm, pcol_hbm, ppup_hbm, up_hbm, down_hbm, left_hbm, right_hbm, endl_hbm, endr_hbm,
    out_hbm, pup_hbm,
    prow, pcol, ppup, vert, side, ends, rows_out, cols_out, pup_out, sem_in, sem_out,
):
    edge = out_in.shape[1]
    tiles = edge // 128
    mid = edge - 2 * BAND
    high_row = edge - BAND
    last = 2 * tiles - 1
    ins = {}

    def get(name, src, dst):
        copy = pltpu.make_async_copy(src, dst, sem_in.at[len(ins)])
        copy.start()
        ins[name] = copy

    verts = (up_hbm, down_hbm)
    sides = (left_hbm, right_hbm)
    for d in range(2):
        get(("side", d), sides[d], side.at[d])
        get(("ends", d), (endl_hbm, endr_hbm)[d], ends.at[d])
    for t in range(2):
        get(("vert", t), verts[t], vert.at[t])
        get(("prow", t), prow_hbm.at[t], prow.at[t])
    for d in range(2):
        get(("pcol", d), pcol_hbm.at[d], pcol.at[d])
    get("ppup", ppup_hbm, ppup)
    outs = []

    def put(src, dst):
        copy = pltpu.make_async_copy(src, dst, sem_out.at[len(outs)])
        copy.start()
        outs.append(copy)

    ins["ends", 0].wait()
    ins["ends", 1].wait()
    for t in range(2):
        ins["vert", t].wait()
        ins["prow", t].wait()
        first = t * high_row
        for c in range(2):
            for k in range(2 * tiles):
                sub = vert[t, c, :, pl.ds(k * 128, 128)].astype(F32)
                if k == tiles - 1 or k == tiles:
                    sub = sub + vert[t, c, :, pl.ds((2 * tiles - 1 - k) * 128, 128)].astype(F32)
                if k == 0 or k == last:
                    d = 0 if k == 0 else 1
                    far = vert[t, c, :, pl.ds(2 * edge + 4 * W + d * BAND, BAND)].astype(F32)
                    sub = sub + (far + ends[d, c, pl.ds(t * BAND, BAND), :].astype(F32))
                rows_out[t, c, :, pl.ds(k * 128, 128)] = (prow[t, c, k] - 0.5 * sub).astype(BF)
            put(rows_out.at[t, c], out_hbm.at[c, pl.ds(first, BAND), :])
    for d in range(2):
        ins["side", d].wait()
        ins["pcol", d].wait()
        for c in range(2):
            sub = side[d, c, pl.ds(0, mid), :].astype(F32)
            cols_out[d, c] = (pcol[d, c] - 0.5 * sub).astype(BF)
            put(cols_out.at[d, c], out_hbm.at[c, pl.ds(BAND, mid), pl.ds(d * last * 128, 128)])
    ins["ppup"].wait()
    for c in range(2):
        for half in range(2):
            rows = pl.ds(half * 128, 128)
            for q in range(4):
                cols = pl.ds(q * 128, 128)
                d = q // 2
                sub = side[d, c, pl.ds(mid + (q % 2) * W + half * 128, 128), :].astype(F32)
                for t in range(2):
                    sub = sub + vert[t, c, :, pl.ds(2 * edge + half * 512 + q * 128, 128)].astype(F32)
                pup_out[c, rows, cols] = ppup[c, rows, cols] - 0.5 * sub
    put(pup_out, pup_hbm)
    for copy in outs:
        copy.wait()


def finish(out, prow, pcol, ppup, ups, sides, ends):
    edge = out.shape[1]
    tiles = edge // 128
    mid = edge - 2 * BAND
    hbm = pl.BlockSpec(memory_space=pl.ANY)
    return pl.pallas_call(
        finish_kernel,
        out_shape=(
            jax.ShapeDtypeStruct(out.shape, BF),
            jax.ShapeDtypeStruct(ppup.shape, F32),
        ),
        in_specs=[hbm] * 10,
        out_specs=(hbm, hbm),
        input_output_aliases={0: 0},
        scratch_shapes=[
            pltpu.VMEM(prow.shape, F32),
            pltpu.VMEM(pcol.shape, F32),
            pltpu.VMEM(ppup.shape, F32),
            pltpu.VMEM((2,) + ups[0].shape, BF),
            pltpu.VMEM((2,) + sides[0].shape, BF),
            pltpu.VMEM((2,) + ends[0].shape, BF),
            pltpu.VMEM((2, 2, BAND, 2 * edge), BF),
            pltpu.VMEM((2, 2, mid, 128), BF),
            pltpu.VMEM(ppup.shape, F32),
            pltpu.SemaphoreType.DMA((16,)),
            pltpu.SemaphoreType.DMA((9,)),
        ],
        compiler_params=pltpu.CompilerParams(vmem_limit_bytes=FINISH_VMEM),
        cost_estimate=pl.CostEstimate(flops=10_000_000, bytes_accessed=17_000_000, transcendentals=0),
        name="shared_bands",
    )(out, prow, pcol, ppup, *ups, *sides, *ends)


def pack_kernel(spec_hbm, pup_hbm, left_c, right_c, left, right, top, bottom, sem):
    edge, wide = spec_hbm.shape[1], spec_hbm.shape[2]
    mid = edge - 2 * BAND
    copies = []

    def put(src, dst):
        copy = pltpu.make_async_copy(src, dst, sem.at[len(copies)])
        copy.start()
        copies.append(copy)

    for ends, msg, first, half in ((left_c, left, 0, 0), (right_c, right, wide - BAND, 1)):
        cols = pl.ds(first, BAND)
        put(spec_hbm.at[:, pl.ds(0, BAND), cols], ends.at[:, pl.ds(0, BAND), :])
        put(spec_hbm.at[:, pl.ds(edge - BAND, BAND), cols], ends.at[:, pl.ds(BAND, BAND), :])
        put(spec_hbm.at[:, pl.ds(BAND, mid), cols], msg.at[:, pl.ds(0, mid), :])
        for q in range(2):
            put(pup_hbm.at[:, :, pl.ds(half * W + q * 128, 128)], msg.at[:, pl.ds(mid + q * W, W), :])
    for msg, first in ((top, 0), (bottom, edge - BAND)):
        put(spec_hbm.at[:, pl.ds(first, BAND), :], msg.at[:, :, pl.ds(0, wide)])
        for q in range(2):
            put(pup_hbm.at[:, pl.ds(q * 128, 128), :], msg.at[:, :, pl.ds(wide + q * 2 * W, 2 * W)])
    for copy in copies:
        copy.wait()


def pack(spectrum, pupils):
    edge, wide = spectrum.shape[1], spectrum.shape[2]
    hbm = pl.BlockSpec(memory_space=pl.ANY)
    ends = jax.ShapeDtypeStruct((2, 2 * BAND, BAND), BF)
    side = jax.ShapeDtypeStruct((2, edge - 2 * BAND + 2 * W, BAND), BF)
    vert = jax.ShapeDtypeStruct((2, BAND, wide + 4 * W + 2 * BAND), BF)
    return pl.pallas_call(
        pack_kernel,
        out_shape=(ends, ends, side, side, vert, vert),
        in_specs=[hbm, hbm],
        out_specs=(hbm,) * 6,
        scratch_shapes=[pltpu.SemaphoreType.DMA((16,))],
        compiler_params=pltpu.CompilerParams(vmem_limit_bytes=PACK_VMEM),
        cost_estimate=pl.CostEstimate(flops=1, bytes_accessed=11_000_000, transcendentals=0),
        name="pack",
    )(spectrum, pupils)


def corners_kernel(top_in, bottom_in, left, right, top, bottom, sem):
    start = top.shape[2] - 2 * BAND
    copies = []
    for t, msg in enumerate((top, bottom)):
        for d, src in enumerate((left, right)):
            copy = pltpu.make_async_copy(
                src.at[:, pl.ds(t * BAND, BAND), :], msg.at[:, :, pl.ds(start + d * BAND, BAND)], sem.at[2 * t + d]
            )
            copy.start()
            copies.append(copy)
    for copy in copies:
        copy.wait()


def add_corners(top, bottom, left, right):
    hbm = pl.BlockSpec(memory_space=pl.ANY)
    vert = jax.ShapeDtypeStruct(top.shape, BF)
    return pl.pallas_call(
        corners_kernel,
        out_shape=(vert, vert),
        in_specs=[hbm] * 4,
        out_specs=(hbm, hbm),
        input_output_aliases={0: 0, 1: 1},
        scratch_shapes=[pltpu.SemaphoreType.DMA((4,))],
        compiler_params=pltpu.CompilerParams(vmem_limit_bytes=CORNER_VMEM),
        cost_estimate=pl.CostEstimate(flops=1, bytes_accessed=1_000_000, transcendentals=0),
        name="add_corners",
    )(top, bottom, left, right)


def local(spectrum, pupils, amplitudes, crop_starts, led_counts):
    rows = lax.axis_size("sy")
    cols = lax.axis_size("sx")
    row = lax.axis_index("sy")
    col = lax.axis_index("sx")

    def chain(count, step):
        return [(i, i + step) for i in range(count) if 0 <= i + step < count]

    left_c, right_c, left, right, top, bottom = pack(spectrum, pupils)
    ends_left = lax.ppermute(right_c, "sx", chain(cols, 1))
    ends_right = lax.ppermute(left_c, "sx", chain(cols, -1))
    from_left = lax.ppermute(right, "sx", chain(cols, 1))
    from_right = lax.ppermute(left, "sx", chain(cols, -1))
    top, bottom = add_corners(top, bottom, ends_left, ends_right)
    from_up = lax.ppermute(bottom, "sy", chain(rows, 1))
    from_down = lax.ppermute(top, "sy", chain(rows, -1))
    weights = jnp.stack([row > 0, row < rows - 1, col > 0, col < cols - 1]).astype(F32)
    out, prow, pcol, ppup = compute(
        spectrum, pupils, amplitudes, crop_starts.reshape(-1), led_counts.reshape(-1), weights
    )
    return finish(out, prow, pcol, ppup, (from_up, from_down), (from_left, from_right), (ends_left, ends_right))


def solution(mesh):
    placed = (
        P(None, "sy", "sx"),
        P(None, "sy", "sx"),
        P("sy", "sx", None, None, None),
        P("sy", "sx", None, None),
        P("sy", "sx"),
    )
    return jax.shard_map(
        local,
        mesh=mesh,
        in_specs=placed,
        out_specs=(P(None, "sy", "sx"), P(None, "sy", "sx")),
        check_vma=False,
    )
```

```python
import functools
import math

import jax
import jax.numpy as jnp
import ml_dtypes
import numpy as np
from jax import lax
from jax.experimental import pallas as pl
from jax.experimental.pallas import tpu as pltpu
from jax.sharding import PartitionSpec as P

H = 64
MAXL = 4
W = 256
HALF = 128
FLOOR_SQUARE = 0.0625
PACK_VMEM = 60 * 1024 * 1024
CORNER_VMEM = 8 * 1024 * 1024
FINISH_VMEM = 66500000
BAND = 2 * H
BF = jnp.bfloat16
F32 = jnp.float32


def halves(table):
    high = table.astype(ml_dtypes.bfloat16)
    low = (table - high.astype(np.float64)).astype(ml_dtypes.bfloat16)
    return high, low


def tables():
    m = np.arange(HALF)[:, None]
    j = np.arange(HALF)[None, :]
    out = []
    for parity in (0, 1):
        phase = ((2 * m + parity) * j % W) * (2.0 * math.pi / W)
        re = np.cos(phase) / math.sqrt(W)
        im = np.sin(phase) / math.sqrt(W)
        left = np.block([[re, -im], [im, re]])
        out.append(left)
        out.append(left.T)
    packed = np.stack([np.stack([halves(t)[part] for t in out]) for part in (0, 1)])
    spread = np.zeros((W, W))
    for p in (0, 1):
        for q in range(HALF):
            spread[2 * q + p, p * HALF + q] = 1.0
    spread = np.concatenate([spread, spread]).astype(ml_dtypes.bfloat16)
    return packed, spread


def split(value):
    high = value.astype(BF)
    low = (value - high.astype(F32)).astype(BF)
    return high, low


def dot(a, b):
    return jnp.dot(a, b, preferred_element_type=F32)


def put_rows(ref, index, rows, cols, value):
    high, low = split(value)
    ref[index, pl.ds(rows, 16), cols] = high
    ref[index, pl.ds(W + rows, 16), cols] = low
    ref[index, pl.ds(2 * W + rows, 16), cols] = high


def put_cols(ref, index, rows, cols, value):
    high, low = split(value)
    ref[index, rows, pl.ds(cols, 128)] = high
    ref[index, rows, pl.ds(W + cols, 128)] = low
    ref[index, rows, pl.ds(2 * W + cols, 128)] = high


def compute_kernel(
    starts, counts, weights, spec_hbm, pup_hbm, amp_hbm, tab_hbm, spread_hbm,
    out_hbm, prow_hbm, pcol_hbm, ppup_hbm,
    spec, pupb, pup, amp, tab_l, tab_r, spread, acc, pacc, inner,
    win, prs, xr, xc, xa, ya, yb, ampq, sem_in, sem_out,
):
    edge = spec.shape[2]
    tiles = edge // 128
    low_row, high_row = BAND, edge - BAND
    mid = high_row - low_row
    copies = []

    def get(src, dst):
        copy = pltpu.make_async_copy(src, dst, sem_in.at[len(copies)])
        copy.start()
        copies.append(copy)

    get(pup_hbm, pupb)
    for h in range(2):
        get(amp_hbm.at[0, :, :, :, pl.ds(h * 128, 128)], amp.at[:, :, h])
    for i, part in enumerate((0, 0, 1)):
        get(tab_hbm.at[part], tab_l.at[:, :, pl.ds(i * W, W)])
        get(tab_hbm.at[part], tab_r.at[:, pl.ds(i * W, W), :])
    get(spread_hbm, spread)
    for g in range(2):
        get(spec_hbm.at[:, :, pl.ds(g * edge, edge)], spec.at[g])

    zero = jnp.zeros((128, 128), F32)

    def clear(i, carry):
        for g in range(2):
            for c in range(2):
                for k in range(tiles):
                    acc[g, c, k, pl.ds(pl.multiple_of(i * 32, 32), 32), :] = zero[:32]
        return carry

    lax.fori_loop(0, edge // 32, clear, 0)
    for c in copies[:-2]:
        c.wait()
    for g in range(2):
        for c in range(2):
            pup[g, c] = pupb[c, :, pl.ds(g * W, W)].astype(F32)
            pacc[g, c] = jnp.zeros((W, W), F32)
    copies[-2].wait()
    copies[-1].wait()
    lane = lax.broadcasted_iota(jnp.int32, (16, 128), 1)

    def slot_stages(g, slot):
        a = starts[(g * MAXL + slot) * 2]
        b = starts[(g * MAXL + slot) * 2 + 1]
        a0 = pl.multiple_of(jnp.minimum(a // 16 * 16, edge - W - 16), 16)
        off = a - a0
        k0 = jnp.minimum(b // 128, tiles - 3)
        s = b - k0 * 128
        sr = lax.rem(s, 128)
        back_shift = lax.rem(128 - sr, 128)
        from_first = lane >= s
        keep_low = lane < 128 - s
        col0 = pl.multiple_of(k0 * 128, 128)
        for c in range(2):
            for r in range(0, W + 16, 16):
                block = spec[g, c, pl.ds(a0 + r, 16), pl.ds(col0, 384)].astype(F32)
                for i in range(3):
                    win[g, c, i, pl.ds(r, 16), :] = block[:, i * 128 : (i + 1) * 128]
        for c in range(2):
            for r in range(0, W, 16):
                r0 = pltpu.roll(pup[g, c, pl.ds(r, 16), pl.ds(0, 128)], sr, 1)
                r1 = pltpu.roll(pup[g, c, pl.ds(r, 16), pl.ds(128, 128)], sr, 1)
                prs[g, c, 0, pl.ds(r, 16), :] = jnp.where(from_first, r0, r1)
                prs[g, c, 1, pl.ds(r, 16), :] = jnp.where(from_first, r1, r0)

        def crop(c, h, r):
            if h == 1:
                return win[g, c, 1, pl.ds(off + r, 16), :]
            return jnp.where(from_first, win[g, c, 0, pl.ds(off + r, 16), :], win[g, c, 2, pl.ds(off + r, 16), :])

        for p in range(2):
            for h in range(2):
                rows = amp[g, slot, h, pl.ds(p, 128, stride=2), :]
                hi, lo = split(rows)
                xa[g, pl.ds(p * 128, 128), pl.ds(h * 128, 128)] = hi
                xa[g, pl.ds(p * 128, 128), pl.ds(W + h * 128, 128)] = lo
        ampq[g] = dot(xa[g], spread[...])
        yield

        for r in range(0, HALF, 16):
            for h in range(2):
                parts = []
                for rr in (r, r + HALF):
                    cr = crop(0, h, rr)
                    ci = crop(1, h, rr)
                    pr = prs[g, 0, h, pl.ds(rr, 16), :]
                    pi = prs[g, 1, h, pl.ds(rr, 16), :]
                    parts.append((pr * cr - pi * ci, pr * ci + pi * cr))
                for c in range(2):
                    cols = pl.ds(h * 128, 128)
                    put_rows(xr.at[g], 0, c * HALF + r, cols, parts[0][c] + parts[1][c])
                    put_rows(xr.at[g], 1, c * HALF + r, cols, parts[0][c] - parts[1][c])
        for q in range(2):
            ya[g, q] = dot(tab_l[2 * q], xr[g, q])
        yield
        for q in range(2):
            for r in range(0, HALF, 16):
                rows = pl.ds(q * HALF + r, 16)
                for c in range(2):
                    y0 = ya[g, q, pl.ds(c * HALF + r, 16), pl.ds(0, 128)]
                    y1 = ya[g, q, pl.ds(c * HALF + r, 16), pl.ds(128, 128)]
                    put_cols(xc.at[g], 0, rows, c * 128, y0 + y1)
                    put_cols(xc.at[g], 1, rows, c * 128, y0 - y1)
        for u in range(2):
            yb[g, u] = dot(xc[g, u], tab_r[2 * u + 1])
        yield
        for u in range(2):
            for r in range(0, W, 16):
                rows = pl.ds(r, 16)
                re = yb[g, u, rows, pl.ds(0, 128)]
                im = yb[g, u, rows, pl.ds(128, 128)]
                power = jnp.maximum(re * re + im * im, FLOOR_SQUARE)
                keeper = 1.0 - ampq[g, rows, pl.ds(u * 128, 128)] * lax.rsqrt(power)
                put_cols(xc.at[g], u, rows, 0, re * keeper)
                put_cols(xc.at[g], u, rows, 128, im * keeper)
        for u in range(2):
            ya[g, u] = dot(xc[g, u], tab_r[2 * u])
        yield
        for q in range(2):
            for r in range(0, HALF, 16):
                rows = pl.ds(q * HALF + r, 16)
                for c in range(2):
                    e = ya[g, 0, rows, pl.ds(c * 128, 128)]
                    o = ya[g, 1, rows, pl.ds(c * 128, 128)]
                    put_rows(xr.at[g], q, c * HALF + r, pl.ds(0, 128), e + o)
                    put_rows(xr.at[g], q, c * HALF + r, pl.ds(128, 128), e - o)
        for q in range(2):
            yb[g, q] = dot(tab_l[2 * q + 1], xr[g, q])
        yield
        for r in range(0, HALF, 16):
            for rr in (r, r + HALF):
                rows = pl.ds(a + rr, 16)
                old = [[acc[g, c, k0 + i, rows, :] for i in range(3)] for c in range(2)]
                drop, terms = [], []
                for h in range(2):
                    back = []
                    for c in range(2):
                        e = yb[g, 0, pl.ds(c * HALF + r, 16), pl.ds(h * 128, 128)]
                        o = yb[g, 1, pl.ds(c * HALF + r, 16), pl.ds(h * 128, 128)]
                        back.append(e + o if rr == r else e - o)
                    br, bi = back
                    pr = prs[g, 0, h, pl.ds(rr, 16), :]
                    pi = prs[g, 1, h, pl.ds(rr, 16), :]
                    cr = crop(0, h, rr)
                    ci = crop(1, h, rr)
                    drop.append((pr * br + pi * bi, pr * bi - pi * br))
                    terms.append((cr * br + ci * bi, cr * bi - ci * br))
                for c in range(2):
                    acc[g, c, k0, rows, :] = old[c][0] + jnp.where(from_first, drop[0][c], 0.0)
                    acc[g, c, k0 + 1, rows, :] = old[c][1] + drop[1][c]
                    acc[g, c, k0 + 2, rows, :] = old[c][2] + jnp.where(from_first, 0.0, drop[0][c])
                for c in range(2):
                    t0 = pltpu.roll(terms[0][c], back_shift, 1)
                    t1 = pltpu.roll(terms[1][c], back_shift, 1)
                    pacc[g, c, pl.ds(rr, 16), pl.ds(0, 128)] += jnp.where(keep_low, t0, t1)
                    pacc[g, c, pl.ds(rr, 16), pl.ds(128, 128)] += jnp.where(keep_low, t1, t0)

    up, down, left_out, right_out = weights[0], weights[1], weights[2], weights[3]
    pending = []

    def put(src, dst):
        copy = pltpu.make_async_copy(src, dst, sem_out.at[len(pending)])
        copy.start()
        pending.append(copy)

    def run(segments):
        def step(slot, carry):
            stages = [slot_stages(g, slot) for g in segments]
            while stages:
                stages = [stage for stage in stages if next(stage, stage) is not stage]
            return carry

        return step

    both = jnp.minimum(counts[0], counts[1])
    lax.fori_loop(0, both, run((0, 1)), 0)
    for g in range(2):
        lax.fori_loop(both, counts[g], run((g,)), 0)
    for g in range(2):
        left = left_out if g == 0 else F32(1.0)
        right = right_out if g == 1 else F32(1.0)
        neighbours = up + down + left + right
        for c in range(2):
            pacc[g, c] = pacc[g, c] + 0.5 * (neighbours * pup[g, c] - pup[1 - g, c])
            put(pacc.at[g, c], ppup_hbm.at[c, :, pl.ds(g * W, W)])
        for c in range(2):
            for k in range(tiles):
                side = left if k == 0 else right if k == tiles - 1 else None
                local = (k == 0 and g == 1) or (k == tiles - 1 and g == 0)
                for t, (first, vert) in enumerate(((0, up), (high_row, down))):
                    factor = vert if side is None else (1.0 + vert) * (1.0 + side) - 1.0
                    own = spec[g, c, pl.ds(first, BAND), pl.ds(k * 128, 128)].astype(F32)
                    add = (0.5 * factor) * own
                    if local:
                        other = spec[1 - g, c, pl.ds(first, BAND), pl.ds((tiles - 1 - k) * 128, 128)].astype(F32)
                        add = add - 0.5 * other
                    acc[g, c, k, pl.ds(first, BAND), :] += add
            for t, first in enumerate((0, high_row)):
                put(acc.at[g, c, :, pl.ds(first, BAND), :], prow_hbm.at[t, c, pl.ds(g * tiles, tiles)])
        k_out = 0 if g == 0 else tiles - 1
        w_out = left_out if g == 0 else right_out
        for c in range(2):

            def outer(i, carry, c=c):
                rows = pl.ds(pl.multiple_of(low_row + i * 128, 128), 128)
                acc[g, c, k_out, rows, :] += (0.5 * w_out) * spec[g, c, rows, pl.ds(k_out * 128, 128)].astype(F32)
                return carry

            lax.fori_loop(0, mid // 128, outer, 0)
            put(acc.at[g, c, k_out, pl.ds(low_row, mid), :], pcol_hbm.at[g, c])
        k_in = tiles - 1 if g == 0 else 0
        first_tile = 1 if g == 0 else 0
        for c in range(2):

            def finish(i, carry, c=c):
                rows = pl.ds(pl.multiple_of(low_row + i * 64, 64), 64)
                dst = pl.ds(pl.multiple_of(i * 64, 64), 64)
                for k in range(first_tile, first_tile + tiles - 1):
                    v = acc[g, c, k, rows, :]
                    if k == k_in:
                        own = spec[g, c, rows, pl.ds(k * 128, 128)].astype(F32)
                        other = spec[1 - g, c, rows, pl.ds((tiles - 1 - k) * 128, 128)].astype(F32)
                        v = v + 0.5 * (own - other)
                    inner[g, c, dst, pl.ds((k - first_tile) * 128, 128)] = v.astype(BF)
                return carry

            lax.fori_loop(0, mid // 64, finish, 0)
            put(
                inner.at[g, c],
                out_hbm.at[c, pl.ds(low_row, mid), pl.ds((g * tiles + first_tile) * 128, (tiles - 1) * 128)],
            )
    for copy in pending:
        copy.wait()


def compute(spectrum, pupils, amplitudes, starts, counts, weights):
    edge = spectrum.shape[1]
    tiles = edge // 128
    mid = edge - 2 * BAND
    packed, spread = tables()
    hbm = pl.BlockSpec(memory_space=pl.ANY)
    smem = pl.BlockSpec(memory_space=pltpu.SMEM)
    return pl.pallas_call(
        compute_kernel,
        out_shape=(
            jax.ShapeDtypeStruct(spectrum.shape, BF),
            jax.ShapeDtypeStruct((2, 2, 2 * tiles, BAND, 128), F32),
            jax.ShapeDtypeStruct((2, 2, mid, 128), F32),
            jax.ShapeDtypeStruct(pupils.shape, F32),
        ),
        in_specs=[smem, smem, smem] + [hbm] * 5,
        out_specs=(hbm, hbm, hbm, hbm),
        scratch_shapes=[
            pltpu.VMEM((2, 2, edge, edge), BF),
            pltpu.VMEM((2, W, 2 * W), BF),
            pltpu.VMEM((2, 2, W, W), F32),
            pltpu.VMEM((2, MAXL, 2, W, 128), F32),
            pltpu.VMEM((4, W, 3 * W), BF),
            pltpu.VMEM((4, 3 * W, W), BF),
            pltpu.VMEM((2 * W, W), BF),
            pltpu.VMEM((2, 2, tiles, edge, 128), F32),
            pltpu.VMEM((2, 2, W, W), F32),
            pltpu.VMEM((2, 2, mid, (tiles - 1) * 128), BF),
            pltpu.VMEM((2, 2, 3, W + 16, 128), F32),
            pltpu.VMEM((2, 2, 2, W, 128), F32),
            pltpu.VMEM((2, 2, 3 * W, W), BF),
            pltpu.VMEM((2, 2, W, 3 * W), BF),
            pltpu.VMEM((2, W, 2 * W), BF),
            pltpu.VMEM((2, 2, W, W), F32),
            pltpu.VMEM((2, 2, W, W), F32),
            pltpu.VMEM((2, W, W), F32),
            pltpu.SemaphoreType.DMA((12,)),
            pltpu.SemaphoreType.DMA((20,)),
        ],
        compiler_params=pltpu.CompilerParams(vmem_limit_bytes=66500000),
        cost_estimate=pl.CostEstimate(flops=20_000_000_000, bytes_accessed=30_000_000, transcendentals=0),
        name="data_terms",
    )(starts, counts, weights, spectrum, pupils, amplitudes, jnp.asarray(packed), jnp.asarray(spread))


def finish_kernel(
    par, out_in, prow_hbm, pcol_hbm, ppup_hbm, verte_hbm, verto_hbm, sidee_hbm, sideo_hbm, endse_hbm, endso_hbm,
    out_hbm, pup_hbm,
    prow, pcol, ppup, vert, side, ends, rows_out, cols_out, pup_out, sem_in, sem_out,
):
    edge = out_in.shape[1]
    tiles = edge // 128
    mid = edge - 2 * BAND
    high_row = edge - BAND
    last = 2 * tiles - 1
    ins = {}

    def get(name, src, dst):
        copy = pltpu.make_async_copy(src, dst, sem_in.at[len(ins)])
        copy.start()
        ins[name] = copy

    verts = (verte_hbm, verto_hbm)
    sides = (sidee_hbm, sideo_hbm)
    v_at = (1 - par[0], par[0])
    s_at = (1 - par[1], par[1])
    for d in range(2):
        get(("side", d), sides[d], side.at[d])
        get(("ends", d), (endse_hbm, endso_hbm)[d], ends.at[d])
    for t in range(2):
        get(("vert", t), verts[t], vert.at[t])
    for t in range(2):
        get(("prow", t), prow_hbm.at[t], prow.at[t])
    for d in range(2):
        get(("pcol", d), pcol_hbm.at[d], pcol.at[d])
    get("ppup", ppup_hbm, ppup)
    outs = []

    def put(src, dst):
        copy = pltpu.make_async_copy(src, dst, sem_out.at[len(outs)])
        copy.start()
        outs.append(copy)

    for d in range(2):
        ins["ends", d].wait()
        ins["side", d].wait()
        ins["vert", d].wait()
    for t in range(2):
        ins["prow", t].wait()
        first = t * high_row
        for c in range(2):
            for k in range(2 * tiles):
                sub = vert[v_at[t], c, :, pl.ds(k * 128, 128)].astype(F32)
                if k == tiles - 1 or k == tiles:
                    sub = sub + vert[v_at[t], c, :, pl.ds((2 * tiles - 1 - k) * 128, 128)].astype(F32)
                if k == 0 or k == last:
                    d = 0 if k == 0 else 1
                    far = vert[v_at[t], c, :, pl.ds(2 * edge + 4 * W + d * BAND, BAND)].astype(F32)
                    sub = sub + (far + ends[s_at[d], c, pl.ds(t * BAND, BAND), :].astype(F32))
                rows_out[t, c, :, pl.ds(k * 128, 128)] = (prow[t, c, k] - 0.5 * sub).astype(BF)
            put(rows_out.at[t, c], out_hbm.at[c, pl.ds(first, BAND), :])
    for d in range(2):
        ins["pcol", d].wait()
        for c in range(2):
            sub = side[s_at[d], c, pl.ds(0, mid), :].astype(F32)
            cols_out[d, c] = (pcol[d, c] - 0.5 * sub).astype(BF)
            put(cols_out.at[d, c], out_hbm.at[c, pl.ds(BAND, mid), pl.ds(d * last * 128, 128)])
    ins["ppup"].wait()
    for c in range(2):
        for half in range(2):
            rows = pl.ds(half * 128, 128)
            for q in range(4):
                cols = pl.ds(q * 128, 128)
                d = q // 2
                sub = side[s_at[d], c, pl.ds(mid + (q % 2) * W + half * 128, 128), :].astype(F32)
                for t in range(2):
                    sub = sub + vert[v_at[t], c, :, pl.ds(2 * edge + half * 512 + q * 128, 128)].astype(F32)
                pup_out[c, rows, cols] = ppup[c, rows, cols] - 0.5 * sub
    put(pup_out, pup_hbm)
    for copy in outs:
        copy.wait()


def finish(parity, out, prow, pcol, ppup, ups, sides, ends):
    edge = out.shape[1]
    tiles = edge // 128
    mid = edge - 2 * BAND
    hbm = pl.BlockSpec(memory_space=pl.ANY)
    return pl.pallas_call(
        finish_kernel,
        out_shape=(
            jax.ShapeDtypeStruct(out.shape, BF),
            jax.ShapeDtypeStruct(ppup.shape, F32),
        ),
        in_specs=[pl.BlockSpec(memory_space=pltpu.SMEM)] + [hbm] * 10,
        out_specs=(hbm, hbm),
        input_output_aliases={1: 0},
        scratch_shapes=[
            pltpu.VMEM(prow.shape, F32),
            pltpu.VMEM(pcol.shape, F32),
            pltpu.VMEM(ppup.shape, F32),
            pltpu.VMEM((2,) + ups[0].shape, BF),
            pltpu.VMEM((2,) + sides[0].shape, BF),
            pltpu.VMEM((2,) + ends[0].shape, BF),
            pltpu.VMEM((2, 2, BAND, 2 * edge), BF),
            pltpu.VMEM((2, 2, mid, 128), BF),
            pltpu.VMEM(ppup.shape, F32),
            pltpu.SemaphoreType.DMA((16,)),
            pltpu.SemaphoreType.DMA((9,)),
        ],
        compiler_params=pltpu.CompilerParams(vmem_limit_bytes=FINISH_VMEM),
        cost_estimate=pl.CostEstimate(flops=10_000_000, bytes_accessed=17_000_000, transcendentals=0),
        name="shared_bands",
    )(parity, out, prow, pcol, ppup, *ups, *sides, *ends)


def pack_kernel(
    par, spec_hbm, pup_hbm,
    ends_e, ends_o, side_e, side_o, vert_e, vert_o,
    ends_v, side_v, vert_v, sem_in, sem_out,
):
    edge, wide = spec_hbm.shape[1], spec_hbm.shape[2]
    mid = edge - 2 * BAND
    ins, outs = [], []

    def get(src, dst):
        copy = pltpu.make_async_copy(src, dst, sem_in.at[len(ins)])
        copy.start()
        ins.append(copy)

    def right(i):
        return 1 - par[1] if i == 0 else par[1]

    def low(i):
        return 1 - par[0] if i == 0 else par[0]

    for i in range(2):
        cols = pl.ds(pl.multiple_of(right(i) * (wide - BAND), 128), BAND)
        get(spec_hbm.at[:, pl.ds(0, BAND), cols], ends_v.at[i, :, pl.ds(0, BAND), :])
        get(spec_hbm.at[:, pl.ds(edge - BAND, BAND), cols], ends_v.at[i, :, pl.ds(BAND, BAND), :])
    for i in range(2):
        cols = pl.ds(pl.multiple_of(right(i) * (wide - BAND), 128), BAND)
        get(spec_hbm.at[:, pl.ds(BAND, mid), cols], side_v.at[i, :, pl.ds(0, mid), :])
        for q in range(2):
            half = pl.ds(pl.multiple_of(right(i) * W + q * 128, 128), 128)
            get(pup_hbm.at[:, :, half], side_v.at[i, :, pl.ds(mid + q * W, W), :])
    for i in range(2):
        rows = pl.ds(pl.multiple_of(low(i) * (edge - BAND), 128), BAND)
        get(spec_hbm.at[:, rows, :], vert_v.at[i, :, :, pl.ds(0, wide)])
        for q in range(2):
            get(pup_hbm.at[:, pl.ds(q * 128, 128), :], vert_v.at[i, :, :, pl.ds(wide + q * 2 * W, 2 * W)])
    body = wide + 4 * W
    done = 0
    for ready, src, dst in (
        (4, ends_v.at[0], ends_e),
        (4, ends_v.at[1], ends_o),
        (7, side_v.at[0], side_e),
        (10, side_v.at[1], side_o),
        (13, vert_v.at[0], vert_e.at[:, :, pl.ds(0, body)]),
        (16, vert_v.at[1], vert_o.at[:, :, pl.ds(0, body)]),
    ):
        while done < ready:
            ins[done].wait()
            done += 1
        copy = pltpu.make_async_copy(src, dst, sem_out.at[len(outs)])
        copy.start()
        outs.append(copy)
    for copy in outs:
        copy.wait()


def pack(parity, spectrum, pupils):
    edge, wide = spectrum.shape[1], spectrum.shape[2]
    hbm = pl.BlockSpec(memory_space=pl.ANY)
    smem = pl.BlockSpec(memory_space=pltpu.SMEM)
    ends = (2, 2 * BAND, BAND)
    side = (2, edge - 2 * BAND + 2 * W, BAND)
    vert = (2, BAND, wide + 4 * W + 2 * BAND)
    return pl.pallas_call(
        pack_kernel,
        out_shape=tuple(jax.ShapeDtypeStruct(shape, BF) for shape in (ends, ends, side, side, vert, vert)),
        in_specs=[smem, hbm, hbm],
        out_specs=(hbm,) * 6,
        scratch_shapes=[
            pltpu.VMEM((2,) + ends, BF),
            pltpu.VMEM((2,) + side, BF),
            pltpu.VMEM((2, 2, BAND, wide + 4 * W), BF),
            pltpu.SemaphoreType.DMA((16,)),
            pltpu.SemaphoreType.DMA((6,)),
        ],
        compiler_params=pltpu.CompilerParams(vmem_limit_bytes=PACK_VMEM),
        cost_estimate=pl.CostEstimate(flops=1, bytes_accessed=11_000_000, transcendentals=0),
        name="pack",
    )(parity, spectrum, pupils)


def corners_kernel(par, e_in, o_in, ends_e, ends_o, vert_e, vert_o, sem):
    body = vert_e.shape[2] - 2 * BAND
    copies = []
    for i, msg in enumerate((vert_e, vert_o)):
        low = 1 - par[0] if i == 0 else par[0]
        rows = pl.ds(pl.multiple_of(low * BAND, 128), BAND)
        for j, src in enumerate((ends_e, ends_o)):
            right = 1 - par[1] if j == 0 else par[1]
            cols = pl.ds(pl.multiple_of(body + right * BAND, 128), BAND)
            copy = pltpu.make_async_copy(src.at[:, rows, :], msg.at[:, :, cols], sem.at[2 * i + j])
            copy.start()
            copies.append(copy)
    for copy in copies:
        copy.wait()


def add_corners(parity, vert_e, vert_o, ends_e, ends_o):
    hbm = pl.BlockSpec(memory_space=pl.ANY)
    smem = pl.BlockSpec(memory_space=pltpu.SMEM)
    vert = jax.ShapeDtypeStruct(vert_e.shape, BF)
    return pl.pallas_call(
        corners_kernel,
        out_shape=(vert, vert),
        in_specs=[smem] + [hbm] * 4,
        out_specs=(hbm, hbm),
        input_output_aliases={1: 0, 2: 1},
        scratch_shapes=[pltpu.SemaphoreType.DMA((4,))],
        compiler_params=pltpu.CompilerParams(vmem_limit_bytes=CORNER_VMEM),
        cost_estimate=pl.CostEstimate(flops=1, bytes_accessed=1_000_000, transcendentals=0),
        name="add_corners",
    )(parity, vert_e, vert_o, ends_e, ends_o)


def local(spectrum, pupils, amplitudes, crop_starts, led_counts):
    rows = lax.axis_size("sy")
    cols = lax.axis_size("sx")
    row = lax.axis_index("sy")
    col = lax.axis_index("sx")

    def swap(value, axis, count, first):
        pairs = [(i, i + 1) for i in range(first, count - 1, 2)]
        return lax.ppermute(value, axis, pairs + [(j, i) for i, j in pairs])

    parity = jnp.stack([row % 2, col % 2]).astype(jnp.int32)
    ends_e, ends_o, side_e, side_o, vert_e, vert_o = pack(parity, spectrum, pupils)
    ends_e = swap(ends_e, "sx", cols, 0)
    ends_o = swap(ends_o, "sx", cols, 1)
    side_e = swap(side_e, "sx", cols, 0)
    side_o = swap(side_o, "sx", cols, 1)
    vert_e, vert_o = add_corners(parity, vert_e, vert_o, ends_e, ends_o)
    vert_o = swap(vert_o, "sy", rows, 1)
    vert_e = swap(vert_e, "sy", rows, 0)
    weights = jnp.stack([row > 0, row < rows - 1, col > 0, col < cols - 1]).astype(F32)
    out, prow, pcol, ppup = compute(
        spectrum, pupils, amplitudes, crop_starts.reshape(-1), led_counts.reshape(-1), weights
    )
    return finish(parity, out, prow, pcol, ppup, (vert_e, vert_o), (side_e, side_o), (ends_e, ends_o))


def solution(mesh):
    placed = (
        P(None, "sy", "sx"),
        P(None, "sy", "sx"),
        P("sy", "sx", None, None, None),
        P("sy", "sx", None, None),
        P("sy", "sx"),
    )
    return jax.shard_map(
        local,
        mesh=mesh,
        in_specs=placed,
        out_specs=(P(None, "sy", "sx"), P(None, "sy", "sx")),
        check_vma=False,
    )
```

```python
import functools
import math

import jax
import jax.numpy as jnp
import ml_dtypes
import numpy as np
from jax import lax
from jax.experimental import pallas as pl
from jax.experimental.pallas import tpu as pltpu
from jax.sharding import PartitionSpec as P

H = 64
MAXL = 4
W = 256
HALF = 128
FLOOR_SQUARE = 0.0625
COST_FLOPS = 1000
COST_BYTES = 1000
PACK_VMEM = 60 * 1024 * 1024
FINISH_VMEM = 66500000
BAND = 2 * H
BF = jnp.bfloat16
F32 = jnp.float32


def halves(table):
    high = table.astype(ml_dtypes.bfloat16)
    low = (table - high.astype(np.float64)).astype(ml_dtypes.bfloat16)
    return high, low


def tables():
    m = np.arange(HALF)[:, None]
    j = np.arange(HALF)[None, :]
    out = []
    for parity in (0, 1):
        phase = ((2 * m + parity) * j % W) * (2.0 * math.pi / W)
        re = np.cos(phase) / math.sqrt(W)
        im = np.sin(phase) / math.sqrt(W)
        left = np.block([[re, -im], [im, re]])
        out.append(left)
        out.append(left.T)
    packed = np.stack([np.stack([halves(t)[part] for t in out]) for part in (0, 1)])
    spread = np.zeros((W, W))
    for p in (0, 1):
        for q in range(HALF):
            spread[2 * q + p, p * HALF + q] = 1.0
    spread = np.concatenate([spread, spread]).astype(ml_dtypes.bfloat16)
    return packed, spread


def split(value):
    high = value.astype(BF)
    low = (value - high.astype(F32)).astype(BF)
    return high, low


def dot(a, b):
    return jnp.dot(a, b, preferred_element_type=F32)


def put_rows(ref, index, rows, cols, value):
    high, low = split(value)
    ref[index, pl.ds(rows, 16), cols] = high
    ref[index, pl.ds(W + rows, 16), cols] = low
    ref[index, pl.ds(2 * W + rows, 16), cols] = high


def put_cols(ref, index, rows, cols, value):
    high, low = split(value)
    ref[index, rows, pl.ds(cols, 128)] = high
    ref[index, rows, pl.ds(W + cols, 128)] = low
    ref[index, rows, pl.ds(2 * W + cols, 128)] = high


def compute_kernel(
    starts, counts, spec_hbm, pup_hbm, amp_hbm, tab_hbm, spread_hbm,
    out_hbm, prow_hbm, pcol_hbm, ppup_hbm,
    spec, pupb, pup, amp, tab_l, tab_r, spread, acc, pacc, inner,
    win, prs, xr, xc, xa, ya, yb, ampq, sem_in, sem_out,
):
    edge = spec.shape[2]
    tiles = edge // 128
    low_row, high_row = BAND, edge - BAND
    mid = high_row - low_row
    copies = []

    def get(src, dst):
        copy = pltpu.make_async_copy(src, dst, sem_in.at[len(copies)])
        copy.start()
        copies.append(copy)

    get(pup_hbm, pupb)
    for h in range(2):
        get(amp_hbm.at[0, :, :, :, pl.ds(h * 128, 128)], amp.at[:, :, h])
    for i, part in enumerate((0, 0, 1)):
        get(tab_hbm.at[part], tab_l.at[:, :, pl.ds(i * W, W)])
        get(tab_hbm.at[part], tab_r.at[:, pl.ds(i * W, W), :])
    get(spread_hbm, spread)
    for g in range(2):
        get(spec_hbm.at[:, :, pl.ds(g * edge, edge)], spec.at[g])

    zero = jnp.zeros((128, 128), F32)

    def clear(i, carry):
        for g in range(2):
            for c in range(2):
                for k in range(tiles):
                    acc[g, c, k, pl.ds(pl.multiple_of(i * 32, 32), 32), :] = zero[:32]
        return carry

    lax.fori_loop(0, edge // 32, clear, 0)
    for c in copies[:-2]:
        c.wait()
    for g in range(2):
        for c in range(2):
            pup[g, c] = pupb[c, :, pl.ds(g * W, W)].astype(F32)
            pacc[g, c] = jnp.zeros((W, W), F32)
    copies[-2].wait()
    copies[-1].wait()
    lane = lax.broadcasted_iota(jnp.int32, (16, 128), 1)

    def slot_stages(g, slot):
        a = starts[(g * MAXL + slot) * 2]
        b = starts[(g * MAXL + slot) * 2 + 1]
        a0 = pl.multiple_of(jnp.minimum(a // 16 * 16, edge - W - 16), 16)
        off = a - a0
        k0 = jnp.minimum(b // 128, tiles - 3)
        s = b - k0 * 128
        sr = lax.rem(s, 128)
        back_shift = lax.rem(128 - sr, 128)
        from_first = lane >= s
        keep_low = lane < 128 - s
        col0 = pl.multiple_of(k0 * 128, 128)
        for c in range(2):
            for r in range(0, W + 16, 16):
                block = spec[g, c, pl.ds(a0 + r, 16), pl.ds(col0, 384)].astype(F32)
                for i in range(3):
                    win[g, c, i, pl.ds(r, 16), :] = block[:, i * 128 : (i + 1) * 128]
        for c in range(2):
            for r in range(0, W, 16):
                r0 = pltpu.roll(pup[g, c, pl.ds(r, 16), pl.ds(0, 128)], sr, 1)
                r1 = pltpu.roll(pup[g, c, pl.ds(r, 16), pl.ds(128, 128)], sr, 1)
                prs[g, c, 0, pl.ds(r, 16), :] = jnp.where(from_first, r0, r1)
                prs[g, c, 1, pl.ds(r, 16), :] = jnp.where(from_first, r1, r0)

        def crop(c, h, r):
            if h == 1:
                return win[g, c, 1, pl.ds(off + r, 16), :]
            return jnp.where(from_first, win[g, c, 0, pl.ds(off + r, 16), :], win[g, c, 2, pl.ds(off + r, 16), :])

        for p in range(2):
            for h in range(2):
                rows = amp[g, slot, h, pl.ds(p, 128, stride=2), :]
                hi, lo = split(rows)
                xa[g, pl.ds(p * 128, 128), pl.ds(h * 128, 128)] = hi
                xa[g, pl.ds(p * 128, 128), pl.ds(W + h * 128, 128)] = lo
        ampq[g] = dot(xa[g], spread[...])
        yield

        for r in range(0, HALF, 16):
            for h in range(2):
                parts = []
                for rr in (r, r + HALF):
                    cr = crop(0, h, rr)
                    ci = crop(1, h, rr)
                    pr = prs[g, 0, h, pl.ds(rr, 16), :]
                    pi = prs[g, 1, h, pl.ds(rr, 16), :]
                    parts.append((pr * cr - pi * ci, pr * ci + pi * cr))
                for c in range(2):
                    cols = pl.ds(h * 128, 128)
                    put_rows(xr.at[g], 0, c * HALF + r, cols, parts[0][c] + parts[1][c])
                    put_rows(xr.at[g], 1, c * HALF + r, cols, parts[0][c] - parts[1][c])
        for q in range(2):
            ya[g, q] = dot(tab_l[2 * q], xr[g, q])
        yield
        for q in range(2):
            for r in range(0, HALF, 16):
                rows = pl.ds(q * HALF + r, 16)
                for c in range(2):
                    y0 = ya[g, q, pl.ds(c * HALF + r, 16), pl.ds(0, 128)]
                    y1 = ya[g, q, pl.ds(c * HALF + r, 16), pl.ds(128, 128)]
                    put_cols(xc.at[g], 0, rows, c * 128, y0 + y1)
                    put_cols(xc.at[g], 1, rows, c * 128, y0 - y1)
        for u in range(2):
            yb[g, u] = dot(xc[g, u], tab_r[2 * u + 1])
        yield
        for u in range(2):
            for r in range(0, W, 16):
                rows = pl.ds(r, 16)
                re = yb[g, u, rows, pl.ds(0, 128)]
                im = yb[g, u, rows, pl.ds(128, 128)]
                power = jnp.maximum(re * re + im * im, FLOOR_SQUARE)
                keeper = 1.0 - ampq[g, rows, pl.ds(u * 128, 128)] * lax.rsqrt(power)
                put_cols(xc.at[g], u, rows, 0, re * keeper)
                put_cols(xc.at[g], u, rows, 128, im * keeper)
        for u in range(2):
            ya[g, u] = dot(xc[g, u], tab_r[2 * u])
        yield
        for q in range(2):
            for r in range(0, HALF, 16):
                rows = pl.ds(q * HALF + r, 16)
                for c in range(2):
                    e = ya[g, 0, rows, pl.ds(c * 128, 128)]
                    o = ya[g, 1, rows, pl.ds(c * 128, 128)]
                    put_rows(xr.at[g], q, c * HALF + r, pl.ds(0, 128), e + o)
                    put_rows(xr.at[g], q, c * HALF + r, pl.ds(128, 128), e - o)
        for q in range(2):
            yb[g, q] = dot(tab_l[2 * q + 1], xr[g, q])
        yield
        for r in range(0, HALF, 16):
            for rr in (r, r + HALF):
                rows = pl.ds(a + rr, 16)
                old = [[acc[g, c, k0 + i, rows, :] for i in range(3)] for c in range(2)]
                drop, terms = [], []
                for h in range(2):
                    back = []
                    for c in range(2):
                        e = yb[g, 0, pl.ds(c * HALF + r, 16), pl.ds(h * 128, 128)]
                        o = yb[g, 1, pl.ds(c * HALF + r, 16), pl.ds(h * 128, 128)]
                        back.append(e + o if rr == r else e - o)
                    br, bi = back
                    pr = prs[g, 0, h, pl.ds(rr, 16), :]
                    pi = prs[g, 1, h, pl.ds(rr, 16), :]
                    cr = crop(0, h, rr)
                    ci = crop(1, h, rr)
                    drop.append((pr * br + pi * bi, pr * bi - pi * br))
                    terms.append((cr * br + ci * bi, cr * bi - ci * br))
                for c in range(2):
                    acc[g, c, k0, rows, :] = old[c][0] + jnp.where(from_first, drop[0][c], 0.0)
                    acc[g, c, k0 + 1, rows, :] = old[c][1] + drop[1][c]
                    acc[g, c, k0 + 2, rows, :] = old[c][2] + jnp.where(from_first, 0.0, drop[0][c])
                for c in range(2):
                    t0 = pltpu.roll(terms[0][c], back_shift, 1)
                    t1 = pltpu.roll(terms[1][c], back_shift, 1)
                    pacc[g, c, pl.ds(rr, 16), pl.ds(0, 128)] += jnp.where(keep_low, t0, t1)
                    pacc[g, c, pl.ds(rr, 16), pl.ds(128, 128)] += jnp.where(keep_low, t1, t0)

    def weight(inside):
        return jnp.where(inside, F32(1.0), F32(0.0))

    row, col = lax.axis_index("sy"), lax.axis_index("sx")
    up, down = weight(row > 0), weight(row < lax.axis_size("sy") - 1)
    left_out, right_out = weight(col > 0), weight(col < lax.axis_size("sx") - 1)
    pending = []

    def put(src, dst):
        copy = pltpu.make_async_copy(src, dst, sem_out.at[len(pending)])
        copy.start()
        pending.append(copy)

    def run(segments):
        def step(slot, carry):
            stages = [slot_stages(g, slot) for g in segments]
            while stages:
                stages = [stage for stage in stages if next(stage, stage) is not stage]
            return carry

        return step

    both = jnp.minimum(counts[0], counts[1])
    lax.fori_loop(0, both, run((0, 1)), 0)
    for g in range(2):
        lax.fori_loop(both, counts[g], run((g,)), 0)
    for g in range(2):
        left = left_out if g == 0 else F32(1.0)
        right = right_out if g == 1 else F32(1.0)
        neighbours = up + down + left + right
        for c in range(2):
            pacc[g, c] = pacc[g, c] + 0.5 * (neighbours * pup[g, c] - pup[1 - g, c])
            put(pacc.at[g, c], ppup_hbm.at[c, :, pl.ds(g * W, W)])
        for c in range(2):
            for k in range(tiles):
                side = left if k == 0 else right if k == tiles - 1 else None
                local = (k == 0 and g == 1) or (k == tiles - 1 and g == 0)
                for t, (first, vert) in enumerate(((0, up), (high_row, down))):
                    factor = vert if side is None else (1.0 + vert) * (1.0 + side) - 1.0
                    own = spec[g, c, pl.ds(first, BAND), pl.ds(k * 128, 128)].astype(F32)
                    add = (0.5 * factor) * own
                    if local:
                        other = spec[1 - g, c, pl.ds(first, BAND), pl.ds((tiles - 1 - k) * 128, 128)].astype(F32)
                        add = add - 0.5 * other
                    acc[g, c, k, pl.ds(first, BAND), :] += add
            for t, first in enumerate((0, high_row)):
                put(acc.at[g, c, :, pl.ds(first, BAND), :], prow_hbm.at[t, c, pl.ds(g * tiles, tiles)])
        k_out = 0 if g == 0 else tiles - 1
        w_out = left_out if g == 0 else right_out
        for c in range(2):

            def outer(i, carry, c=c):
                rows = pl.ds(pl.multiple_of(low_row + i * 128, 128), 128)
                acc[g, c, k_out, rows, :] += (0.5 * w_out) * spec[g, c, rows, pl.ds(k_out * 128, 128)].astype(F32)
                return carry

            lax.fori_loop(0, mid // 128, outer, 0)
            put(acc.at[g, c, k_out, pl.ds(low_row, mid), :], pcol_hbm.at[g, c])
        k_in = tiles - 1 if g == 0 else 0
        first_tile = 1 if g == 0 else 0
        for c in range(2):

            def finish(i, carry, c=c):
                rows = pl.ds(pl.multiple_of(low_row + i * 64, 64), 64)
                dst = pl.ds(pl.multiple_of(i * 64, 64), 64)
                for k in range(first_tile, first_tile + tiles - 1):
                    v = acc[g, c, k, rows, :]
                    if k == k_in:
                        own = spec[g, c, rows, pl.ds(k * 128, 128)].astype(F32)
                        other = spec[1 - g, c, rows, pl.ds((tiles - 1 - k) * 128, 128)].astype(F32)
                        v = v + 0.5 * (own - other)
                    inner[g, c, dst, pl.ds((k - first_tile) * 128, 128)] = v.astype(BF)
                return carry

            lax.fori_loop(0, mid // 64, finish, 0)
            put(
                inner.at[g, c],
                out_hbm.at[c, pl.ds(low_row, mid), pl.ds((g * tiles + first_tile) * 128, (tiles - 1) * 128)],
            )
    for copy in pending:
        copy.wait()


def compute(spectrum, pupils, amplitudes, starts, counts):
    edge = spectrum.shape[1]
    tiles = edge // 128
    mid = edge - 2 * BAND
    packed, spread = tables()
    hbm = pl.BlockSpec(memory_space=pl.ANY)
    smem = pl.BlockSpec(memory_space=pltpu.SMEM)
    return pl.pallas_call(
        compute_kernel,
        out_shape=(
            jax.ShapeDtypeStruct(spectrum.shape, BF),
            jax.ShapeDtypeStruct((2, 2, 2 * tiles, BAND, 128), F32),
            jax.ShapeDtypeStruct((2, 2, mid, 128), F32),
            jax.ShapeDtypeStruct(pupils.shape, F32),
        ),
        in_specs=[smem, smem] + [hbm] * 5,
        out_specs=(hbm, hbm, hbm, hbm),
        scratch_shapes=[
            pltpu.VMEM((2, 2, edge, edge), BF),
            pltpu.VMEM((2, W, 2 * W), BF),
            pltpu.VMEM((2, 2, W, W), F32),
            pltpu.VMEM((2, MAXL, 2, W, 128), F32),
            pltpu.VMEM((4, W, 3 * W), BF),
            pltpu.VMEM((4, 3 * W, W), BF),
            pltpu.VMEM((2 * W, W), BF),
            pltpu.VMEM((2, 2, tiles, edge, 128), F32),
            pltpu.VMEM((2, 2, W, W), F32),
            pltpu.VMEM((2, 2, mid, (tiles - 1) * 128), BF),
            pltpu.VMEM((2, 2, 3, W + 16, 128), F32),
            pltpu.VMEM((2, 2, 2, W, 128), F32),
            pltpu.VMEM((2, 2, 3 * W, W), BF),
            pltpu.VMEM((2, 2, W, 3 * W), BF),
            pltpu.VMEM((2, W, 2 * W), BF),
            pltpu.VMEM((2, 2, W, W), F32),
            pltpu.VMEM((2, 2, W, W), F32),
            pltpu.VMEM((2, W, W), F32),
            pltpu.SemaphoreType.DMA((12,)),
            pltpu.SemaphoreType.DMA((20,)),
        ],
        compiler_params=pltpu.CompilerParams(vmem_limit_bytes=66500000),
        cost_estimate=pl.CostEstimate(flops=COST_FLOPS, bytes_accessed=COST_BYTES, transcendentals=0),
        name="data_terms",
    )(starts, counts, spectrum, pupils, amplitudes, jnp.asarray(packed), jnp.asarray(spread))


def finish_kernel(
    out_in, prow_hbm, pcol_hbm, ppup_hbm, verto_hbm, sidee_hbm, sideo_hbm,
    maino_hbm, antio_hbm, maine_hbm, antie_hbm, verte_hbm,
    out_hbm, pup_hbm,
    prow, pcol, ppup, vert, side, diag, rows_out, cols_out, pup_out, sem_in, sem_out,
):
    edge = out_in.shape[1]
    tiles = edge // 128
    mid = edge - 2 * BAND
    high_row = edge - BAND
    last = 2 * tiles - 1
    ins = {}

    def get(name, src, dst):
        copy = pltpu.make_async_copy(src, dst, sem_in.at[len(ins)])
        copy.start()
        ins[name] = copy

    verts = (verte_hbm, verto_hbm)
    sides = (sidee_hbm, sideo_hbm)
    diags = ((maine_hbm, maino_hbm), (antie_hbm, antio_hbm))
    odd_row, odd_col = parity_of("sy"), parity_of("sx")
    v_at = (1 - odd_row, odd_row)
    s_at = (1 - odd_col, odd_col)
    for i in range(2):
        get(("vert", i), verts[i], vert.at[i])
    for c in range(2):
        get(("prow", 0, c), prow_hbm.at[0, c], prow.at[0, c])
    for i in range(2):
        get(("side", i), sides[i], side.at[i])
    for j in range(2):
        for i in range(2):
            get(("diag", j, i), diags[j][i], diag.at[j, i])
    for c in range(2):
        get(("prow", 1, c), prow_hbm.at[1, c], prow.at[1, c])
    for d in range(2):
        get(("pcol", d), pcol_hbm.at[d], pcol.at[d])
    get("ppup", ppup_hbm, ppup)
    outs = []

    def put(src, dst):
        copy = pltpu.make_async_copy(src, dst, sem_out.at[len(outs)])
        copy.start()
        outs.append(copy)

    def band(t, c, k):
        sub = vert[v_at[t], c, :, pl.ds(k * 128, 128)].astype(F32)
        if k == tiles - 1 or k == tiles:
            sub = sub + vert[v_at[t], c, :, pl.ds((2 * tiles - 1 - k) * 128, 128)].astype(F32)
        if k == 0 or k == last:
            d = 0 if k == 0 else 1
            far = diag[0 if t == d else 1, v_at[t], c].astype(F32)
            sub = sub + (far + side[s_at[d], c, pl.ds(t * high_row, BAND), :].astype(F32))
        rows_out[t, c, :, pl.ds(k * 128, 128)] = (prow[t, c, k] - 0.5 * sub).astype(BF)

    for i in range(2):
        ins["vert", i].wait()
    for t in range(2):
        for c in range(2):
            ins["prow", t, c].wait()
            for k in range(1, last):
                band(t, c, k)
        if t == 0:
            for i in range(2):
                ins["side", i].wait()
                for j in range(2):
                    ins["diag", j, i].wait()
        for c in range(2):
            band(t, c, 0)
            band(t, c, last)
            put(rows_out.at[t, c], out_hbm.at[c, pl.ds(t * high_row, BAND), :])
    for d in range(2):
        ins["pcol", d].wait()
        for c in range(2):
            sub = side[s_at[d], c, pl.ds(BAND, mid), :].astype(F32)
            cols_out[d, c] = (pcol[d, c] - 0.5 * sub).astype(BF)
            put(cols_out.at[d, c], out_hbm.at[c, pl.ds(BAND, mid), pl.ds(d * last * 128, 128)])
    ins["ppup"].wait()
    for c in range(2):
        for half in range(2):
            rows = pl.ds(half * 128, 128)
            for q in range(4):
                cols = pl.ds(q * 128, 128)
                d = q // 2
                sub = side[s_at[d], c, pl.ds(edge + (q % 2) * W + half * 128, 128), :].astype(F32)
                for t in range(2):
                    sub = sub + vert[v_at[t], c, :, pl.ds(2 * edge + half * 512 + q * 128, 128)].astype(F32)
                pup_out[c, rows, cols] = ppup[c, rows, cols] - 0.5 * sub
        put(pup_out.at[c], pup_hbm.at[c])
    for copy in outs:
        copy.wait()


def finish(out, prow, pcol, ppup, verts, sides, diags):
    edge = out.shape[1]
    tiles = edge // 128
    mid = edge - 2 * BAND
    hbm = pl.BlockSpec(memory_space=pl.ANY)
    return pl.pallas_call(
        finish_kernel,
        out_shape=(
            jax.ShapeDtypeStruct(out.shape, BF),
            jax.ShapeDtypeStruct(ppup.shape, F32),
        ),
        in_specs=[hbm] * 12,
        out_specs=(hbm, hbm),
        input_output_aliases={0: 0},
        scratch_shapes=[
            pltpu.VMEM(prow.shape, F32),
            pltpu.VMEM(pcol.shape, F32),
            pltpu.VMEM(ppup.shape, F32),
            pltpu.VMEM((2,) + verts[0].shape, BF),
            pltpu.VMEM((2,) + sides[0].shape, BF),
            pltpu.VMEM((2, 2) + diags[0].shape, BF),
            pltpu.VMEM((2, 2, BAND, 2 * edge), BF),
            pltpu.VMEM((2, 2, mid, 128), BF),
            pltpu.VMEM(ppup.shape, F32),
            pltpu.SemaphoreType.DMA((16,)),
            pltpu.SemaphoreType.DMA((10,)),
        ],
        compiler_params=pltpu.CompilerParams(vmem_limit_bytes=FINISH_VMEM),
        cost_estimate=pl.CostEstimate(flops=10_000_000, bytes_accessed=17_000_000, transcendentals=0),
        name="shared_bands",
    )(out, prow, pcol, ppup, verts[1], *sides, diags[1], diags[3], diags[0], diags[2], verts[0])


def parity_of(axis):
    return lax.rem(lax.axis_index(axis), 2)


def pack_kernel(
    spec_hbm, pup_hbm,
    vert_o, side_e, side_o, main_o, anti_o, main_e, anti_e, vert_e,
    vert_v, side_v, diag_v, sem_in, sem_out,
):
    edge, wide = spec_hbm.shape[1], spec_hbm.shape[2]
    odd_row, odd_col = parity_of("sy"), parity_of("sx")
    low = (1 - odd_row, odd_row)
    right = (1 - odd_col, odd_col)
    ins, outs = [], []

    def get(src, dst):
        for c in range(2):
            copy = pltpu.make_async_copy(src.at[c], dst.at[c], sem_in.at[len(ins)])
            copy.start()
            ins.append(copy)

    def first_row(i):
        return pl.ds(pl.multiple_of(low[i] * (edge - BAND), 128), BAND)

    def first_col(flag):
        return pl.ds(pl.multiple_of(flag * (wide - BAND), 128), BAND)

    plan = []
    for i in (1, 0):
        get(spec_hbm.at[:, first_row(i), :], vert_v.at[i, :, :, pl.ds(0, wide)])
        for q in range(2):
            get(pup_hbm.at[:, pl.ds(q * 128, 128), :], vert_v.at[i, :, :, pl.ds(wide + q * 2 * W, 2 * W)])
        plan.append((len(ins), vert_v.at[i], (vert_e, vert_o)[i]))
    for i in (1, 0):
        get(spec_hbm.at[:, :, first_col(right[i])], side_v.at[i, :, pl.ds(0, edge), :])
        for q in range(2):
            half = pl.ds(pl.multiple_of(right[i] * W + q * 128, 128), 128)
            get(pup_hbm.at[:, :, half], side_v.at[i, :, pl.ds(edge + q * W, W), :])
        plan.append((len(ins), side_v.at[i], (side_e, side_o)[i]))
    for j, pair in enumerate(((main_e, main_o), (anti_e, anti_o))):
        for i in range(2):
            flag = low[i] if j == 0 else 1 - low[i]
            get(spec_hbm.at[:, first_row(i), first_col(flag)], diag_v.at[j, i])
            plan.append((len(ins), diag_v.at[j, i], pair[i]))
    done = 0
    for ready, src, dst in plan:
        while done < ready:
            ins[done].wait()
            done += 1
        for c in range(2):
            copy = pltpu.make_async_copy(src.at[c], dst.at[c], sem_out.at[len(outs)])
            copy.start()
            outs.append(copy)
    for copy in outs:
        copy.wait()


def pack(spectrum, pupils):
    edge, wide = spectrum.shape[1], spectrum.shape[2]
    hbm = pl.BlockSpec(memory_space=pl.ANY)
    vert = (2, BAND, wide + 4 * W)
    side = (2, edge + 2 * W, BAND)
    diag = (2, BAND, BAND)
    return pl.pallas_call(
        pack_kernel,
        out_shape=tuple(jax.ShapeDtypeStruct(shape, BF) for shape in (vert, side, side, diag, diag, diag, diag, vert)),
        in_specs=[hbm, hbm],
        out_specs=(hbm,) * 8,
        scratch_shapes=[
            pltpu.VMEM((2,) + vert, BF),
            pltpu.VMEM((2,) + side, BF),
            pltpu.VMEM((2, 2) + diag, BF),
            pltpu.SemaphoreType.DMA((32,)),
            pltpu.SemaphoreType.DMA((16,)),
        ],
        compiler_params=pltpu.CompilerParams(vmem_limit_bytes=PACK_VMEM),
        cost_estimate=pl.CostEstimate(flops=1, bytes_accessed=11_000_000, transcendentals=0),
        name="pack",
    )(spectrum, pupils)


def local(spectrum, pupils, amplitudes, crop_starts, led_counts):
    rows = lax.axis_size("sy")
    cols = lax.axis_size("sx")

    def swap(value, axis, count, first):
        pairs = [(i, i + 1) for i in range(first, count - 1, 2)]
        return lax.ppermute(value, axis, pairs + [(j, i) for i, j in pairs])

    def swap_diagonal(value, first, step):
        pairs = [
            (y * cols + x, (y + 1) * cols + x + step)
            for y in range(first, rows - 1, 2)
            for x in range(cols)
            if 0 <= x + step < cols
        ]
        return lax.ppermute(value, ("sy", "sx"), pairs + [(j, i) for i, j in pairs])

    vert_o, side_e, side_o, main_o, anti_o, main_e, anti_e, vert_e = pack(spectrum, pupils)
    below = swap(vert_o, "sy", rows, 1)
    sides = (swap(side_e, "sx", cols, 0), swap(side_o, "sx", cols, 1))
    diags = (
        swap_diagonal(main_e, 0, 1),
        swap_diagonal(main_o, 1, 1),
        swap_diagonal(anti_e, 0, -1),
        swap_diagonal(anti_o, 1, -1),
    )
    verts = (swap(vert_e, "sy", rows, 0), below)
    out, prow, pcol, ppup = compute(spectrum, pupils, amplitudes, crop_starts.reshape(-1), led_counts.reshape(-1))
    return finish(out, prow, pcol, ppup, verts, sides, diags)


def solution(mesh):
    placed = (
        P(None, "sy", "sx"),
        P(None, "sy", "sx"),
        P("sy", "sx", None, None, None),
        P("sy", "sx", None, None),
        P("sy", "sx"),
    )
    return jax.shard_map(
        local,
        mesh=mesh,
        in_specs=placed,
        out_specs=(P(None, "sy", "sx"), P(None, "sy", "sx")),
        check_vma=False,
    )
```

```python
import functools
import math

import jax
import jax.numpy as jnp
import ml_dtypes
import numpy as np
from jax import lax
from jax.experimental import pallas as pl
from jax.experimental.pallas import tpu as pltpu
from jax.sharding import PartitionSpec as P

H = 64
MAXL = 4
W = 256
HALF = 128
FLOOR_SQUARE = 0.0625
COST_FLOPS = 20_000_000_000
COST_BYTES = 30_000_000
FULL_VMEM = 60 * 1024 * 1024
DATA_VMEM = 53 * 1024 * 1024
FINISH_VMEM = 24 * 1024 * 1024
BAND = 2 * H
BF = jnp.bfloat16
F32 = jnp.float32


def halves(table):
    high = table.astype(ml_dtypes.bfloat16)
    low = (table - high.astype(np.float64)).astype(ml_dtypes.bfloat16)
    return high, low


def tables():
    m = np.arange(HALF)[:, None]
    j = np.arange(HALF)[None, :]
    out = []
    for parity in (0, 1):
        phase = ((2 * m + parity) * j % W) * (2.0 * math.pi / W)
        re = np.cos(phase) / math.sqrt(W)
        im = np.sin(phase) / math.sqrt(W)
        left = np.block([[re, -im], [im, re]])
        out.append(left)
        out.append(left.T)
    packed = np.stack([np.stack([halves(t)[part] for t in out]) for part in (0, 1)])
    spread = np.zeros((W, W))
    for p in (0, 1):
        for q in range(HALF):
            spread[2 * q + p, p * HALF + q] = 1.0
    spread = np.concatenate([spread, spread]).astype(ml_dtypes.bfloat16)
    return packed, spread


def split(value):
    high = value.astype(BF)
    low = (value - high.astype(F32)).astype(BF)
    return high, low


def dot(a, b):
    return jnp.dot(a, b, preferred_element_type=F32)


def put_rows(ref, index, rows, cols, value):
    high, low = split(value)
    ref[index, pl.ds(rows, 16), cols] = high
    ref[index, pl.ds(W + rows, 16), cols] = low
    ref[index, pl.ds(2 * W + rows, 16), cols] = high


def put_cols(ref, index, rows, cols, value):
    high, low = split(value)
    ref[index, rows, pl.ds(cols, 128)] = high
    ref[index, rows, pl.ds(W + cols, 128)] = low
    ref[index, rows, pl.ds(2 * W + cols, 128)] = high


def compute_kernel(
    starts, counts, spec_hbm, pup_hbm, amp_hbm, tab_hbm, spread_hbm,
    out_hbm, prow, pcol, ppup,
    spec, pupb, pup, amp, tab_l, tab_r, spread, acc, pacc,
    win, prs, xr, xc, xa, ya, yb, ampq, sem_in, sem_out,
):
    edge = spec.shape[2]
    tiles = edge // 128
    low_row, high_row = BAND, edge - BAND
    mid = high_row - low_row
    copies = []

    def get(src, dst):
        copy = pltpu.make_async_copy(src, dst, sem_in.at[len(copies)])
        copy.start()
        copies.append(copy)

    get(pup_hbm, pupb)
    for h in range(2):
        get(amp_hbm.at[0, :, :, :, pl.ds(h * 128, 128)], amp.at[:, :, h])
    for i, part in enumerate((0, 0, 1)):
        get(tab_hbm.at[part], tab_l.at[:, :, pl.ds(i * W, W)])
        get(tab_hbm.at[part], tab_r.at[:, pl.ds(i * W, W), :])
    get(spread_hbm, spread)
    for g in range(2):
        get(spec_hbm.at[:, :, pl.ds(g * edge, edge)], spec.at[g])

    zero = jnp.zeros((128, 128), F32)

    def clear(i, carry):
        for g in range(2):
            for c in range(2):
                for k in range(tiles):
                    acc[g, c, k, pl.ds(pl.multiple_of(i * 32, 32), 32), :] = zero[:32]
        return carry

    lax.fori_loop(0, edge // 32, clear, 0)
    for c in copies[:-2]:
        c.wait()
    for g in range(2):
        for c in range(2):
            pup[g, c] = pupb[c, :, pl.ds(g * W, W)].astype(F32)
            pacc[g, c] = jnp.zeros((W, W), F32)
    copies[-2].wait()
    copies[-1].wait()
    lane = lax.broadcasted_iota(jnp.int32, (16, 128), 1)

    def slot_stages(g, slot):
        a = starts[(g * MAXL + slot) * 2]
        b = starts[(g * MAXL + slot) * 2 + 1]
        a0 = pl.multiple_of(jnp.minimum(a // 16 * 16, edge - W - 16), 16)
        off = a - a0
        k0 = jnp.minimum(b // 128, tiles - 3)
        s = b - k0 * 128
        sr = lax.rem(s, 128)
        back_shift = lax.rem(128 - sr, 128)
        from_first = lane >= s
        keep_low = lane < 128 - s
        col0 = pl.multiple_of(k0 * 128, 128)
        for c in range(2):
            for r in range(0, W + 16, 16):
                block = spec[g, c, pl.ds(a0 + r, 16), pl.ds(col0, 384)].astype(F32)
                for i in range(3):
                    win[g, c, i, pl.ds(r, 16), :] = block[:, i * 128 : (i + 1) * 128]
        for c in range(2):
            for r in range(0, W, 16):
                r0 = pltpu.roll(pup[g, c, pl.ds(r, 16), pl.ds(0, 128)], sr, 1)
                r1 = pltpu.roll(pup[g, c, pl.ds(r, 16), pl.ds(128, 128)], sr, 1)
                prs[g, c, 0, pl.ds(r, 16), :] = jnp.where(from_first, r0, r1)
                prs[g, c, 1, pl.ds(r, 16), :] = jnp.where(from_first, r1, r0)

        def crop(c, h, r):
            if h == 1:
                return win[g, c, 1, pl.ds(off + r, 16), :]
            return jnp.where(from_first, win[g, c, 0, pl.ds(off + r, 16), :], win[g, c, 2, pl.ds(off + r, 16), :])

        for p in range(2):
            for h in range(2):
                rows = amp[g, slot, h, pl.ds(p, 128, stride=2), :]
                hi, lo = split(rows)
                xa[g, pl.ds(p * 128, 128), pl.ds(h * 128, 128)] = hi
                xa[g, pl.ds(p * 128, 128), pl.ds(W + h * 128, 128)] = lo
        ampq[g] = dot(xa[g], spread[...])
        yield

        for r in range(0, HALF, 16):
            for h in range(2):
                parts = []
                for rr in (r, r + HALF):
                    cr = crop(0, h, rr)
                    ci = crop(1, h, rr)
                    pr = prs[g, 0, h, pl.ds(rr, 16), :]
                    pi = prs[g, 1, h, pl.ds(rr, 16), :]
                    parts.append((pr * cr - pi * ci, pr * ci + pi * cr))
                for c in range(2):
                    cols = pl.ds(h * 128, 128)
                    put_rows(xr.at[g], 0, c * HALF + r, cols, parts[0][c] + parts[1][c])
                    put_rows(xr.at[g], 1, c * HALF + r, cols, parts[0][c] - parts[1][c])
        for q in range(2):
            ya[g, q] = dot(tab_l[2 * q], xr[g, q])
        yield
        for q in range(2):
            for r in range(0, HALF, 16):
                rows = pl.ds(q * HALF + r, 16)
                for c in range(2):
                    y0 = ya[g, q, pl.ds(c * HALF + r, 16), pl.ds(0, 128)]
                    y1 = ya[g, q, pl.ds(c * HALF + r, 16), pl.ds(128, 128)]
                    put_cols(xc.at[g], 0, rows, c * 128, y0 + y1)
                    put_cols(xc.at[g], 1, rows, c * 128, y0 - y1)
        for u in range(2):
            yb[g, u] = dot(xc[g, u], tab_r[2 * u + 1])
        yield
        for u in range(2):
            for r in range(0, W, 16):
                rows = pl.ds(r, 16)
                re = yb[g, u, rows, pl.ds(0, 128)]
                im = yb[g, u, rows, pl.ds(128, 128)]
                power = jnp.maximum(re * re + im * im, FLOOR_SQUARE)
                keeper = 1.0 - ampq[g, rows, pl.ds(u * 128, 128)] * lax.rsqrt(power)
                put_cols(xc.at[g], u, rows, 0, re * keeper)
                put_cols(xc.at[g], u, rows, 128, im * keeper)
        for u in range(2):
            ya[g, u] = dot(xc[g, u], tab_r[2 * u])
        yield
        for q in range(2):
            for r in range(0, HALF, 16):
                rows = pl.ds(q * HALF + r, 16)
                for c in range(2):
                    e = ya[g, 0, rows, pl.ds(c * 128, 128)]
                    o = ya[g, 1, rows, pl.ds(c * 128, 128)]
                    put_rows(xr.at[g], q, c * HALF + r, pl.ds(0, 128), e + o)
                    put_rows(xr.at[g], q, c * HALF + r, pl.ds(128, 128), e - o)
        for q in range(2):
            yb[g, q] = dot(tab_l[2 * q + 1], xr[g, q])
        yield
        for r in range(0, HALF, 16):
            for rr in (r, r + HALF):
                rows = pl.ds(a + rr, 16)
                old = [[acc[g, c, k0 + i, rows, :] for i in range(3)] for c in range(2)]
                drop, terms = [], []
                for h in range(2):
                    back = []
                    for c in range(2):
                        e = yb[g, 0, pl.ds(c * HALF + r, 16), pl.ds(h * 128, 128)]
                        o = yb[g, 1, pl.ds(c * HALF + r, 16), pl.ds(h * 128, 128)]
                        back.append(e + o if rr == r else e - o)
                    br, bi = back
                    pr = prs[g, 0, h, pl.ds(rr, 16), :]
                    pi = prs[g, 1, h, pl.ds(rr, 16), :]
                    cr = crop(0, h, rr)
                    ci = crop(1, h, rr)
                    drop.append((pr * br + pi * bi, pr * bi - pi * br))
                    terms.append((cr * br + ci * bi, cr * bi - ci * br))
                for c in range(2):
                    acc[g, c, k0, rows, :] = old[c][0] + jnp.where(from_first, drop[0][c], 0.0)
                    acc[g, c, k0 + 1, rows, :] = old[c][1] + drop[1][c]
                    acc[g, c, k0 + 2, rows, :] = old[c][2] + jnp.where(from_first, 0.0, drop[0][c])
                for c in range(2):
                    t0 = pltpu.roll(terms[0][c], back_shift, 1)
                    t1 = pltpu.roll(terms[1][c], back_shift, 1)
                    pacc[g, c, pl.ds(rr, 16), pl.ds(0, 128)] += jnp.where(keep_low, t0, t1)
                    pacc[g, c, pl.ds(rr, 16), pl.ds(128, 128)] += jnp.where(keep_low, t1, t0)

    def weight(inside):
        return jnp.where(inside, F32(1.0), F32(0.0))

    row, col = lax.axis_index("sy"), lax.axis_index("sx")
    up, down = weight(row > 0), weight(row < lax.axis_size("sy") - 1)
    left_out, right_out = weight(col > 0), weight(col < lax.axis_size("sx") - 1)
    pending = []

    def put(src, dst):
        copy = pltpu.make_async_copy(src, dst, sem_out.at[len(pending)])
        copy.start()
        pending.append(copy)

    def run(segments):
        def step(slot, carry):
            stages = [slot_stages(g, slot) for g in segments]
            while stages:
                stages = [stage for stage in stages if next(stage, stage) is not stage]
            return carry

        return step

    both = jnp.minimum(counts[0], counts[1])
    lax.fori_loop(0, both, run((0, 1)), 0)
    for g in range(2):
        lax.fori_loop(both, counts[g], run((g,)), 0)
    for c in range(2):

        def finish(i, carry, c=c):
            rows = pl.ds(pl.multiple_of(low_row + i * 64, 64), 64)
            for k in range(1, tiles - 1):
                for g in range(2):
                    spec[g, c, rows, pl.ds(k * 128, 128)] = acc[g, c, k, rows, :].astype(BF)
            end = pl.ds((tiles - 1) * 128, 128)
            start = pl.ds(0, 128)
            gap = 0.5 * (spec[0, c, rows, end].astype(F32) - spec[1, c, rows, start].astype(F32))
            spec[0, c, rows, end] = (acc[0, c, tiles - 1, rows, :] + gap).astype(BF)
            spec[1, c, rows, start] = (acc[1, c, 0, rows, :] - gap).astype(BF)
            return carry

        lax.fori_loop(0, mid // 64, finish, 0)
        for g in range(2):
            first_tile = 1 - g
            cols = (tiles - 1) * 128
            put(
                spec.at[g, c, pl.ds(low_row, mid), pl.ds(first_tile * 128, cols)],
                out_hbm.at[c, pl.ds(low_row, mid), pl.ds((g * tiles + first_tile) * 128, cols)],
            )
    for g in range(2):
        left = left_out if g == 0 else F32(1.0)
        right = right_out if g == 1 else F32(1.0)
        neighbours = up + down + left + right
        for c in range(2):
            ppup[c, :, pl.ds(g * W, W)] = pacc[g, c] + 0.5 * (neighbours * pup[g, c] - pup[1 - g, c])
        for c in range(2):
            for k in range(tiles):
                side = left if k == 0 else right if k == tiles - 1 else None
                local = (k == 0 and g == 1) or (k == tiles - 1 and g == 0)
                for t, (first, vert) in enumerate(((0, up), (high_row, down))):
                    factor = vert if side is None else (1.0 + vert) * (1.0 + side) - 1.0
                    own = spec[g, c, pl.ds(first, BAND), pl.ds(k * 128, 128)].astype(F32)
                    add = (0.5 * factor) * own
                    if local:
                        other = spec[1 - g, c, pl.ds(first, BAND), pl.ds((tiles - 1 - k) * 128, 128)].astype(F32)
                        add = add - 0.5 * other
                    prow[t, c, g * tiles + k] = acc[g, c, k, pl.ds(first, BAND), :] + add
        k_out = 0 if g == 0 else tiles - 1
        w_out = left_out if g == 0 else right_out
        for c in range(2):

            def outer(i, carry, c=c):
                rows = pl.ds(pl.multiple_of(low_row + i * 128, 128), 128)
                add = (0.5 * w_out) * spec[g, c, rows, pl.ds(k_out * 128, 128)].astype(F32)
                pcol[g, c, pl.ds(pl.multiple_of(i * 128, 128), 128), :] = acc[g, c, k_out, rows, :] + add
                return carry

            lax.fori_loop(0, mid // 128, outer, 0)
    for copy in pending:
        copy.wait()


def compute(spectrum, pupils, amplitudes, starts, counts):
    edge = spectrum.shape[1]
    tiles = edge // 128
    mid = edge - 2 * BAND
    packed, spread = tables()
    hbm = pl.BlockSpec(memory_space=pl.ANY)
    smem = pl.BlockSpec(memory_space=pltpu.SMEM)
    vmem = pl.BlockSpec(memory_space=pltpu.VMEM)
    return pl.pallas_call(
        compute_kernel,
        out_shape=(
            jax.ShapeDtypeStruct(spectrum.shape, BF),
            pltpu.VMEM((2, 2, 2 * tiles, BAND, 128), F32),
            pltpu.VMEM((2, 2, mid, 128), F32),
            pltpu.VMEM(pupils.shape, F32),
        ),
        in_specs=[smem, smem] + [hbm] * 5,
        out_specs=(hbm, vmem, vmem, vmem),
        scratch_shapes=[
            pltpu.VMEM((2, 2, edge, edge), BF),
            pltpu.VMEM((2, W, 2 * W), BF),
            pltpu.VMEM((2, 2, W, W), F32),
            pltpu.VMEM((2, MAXL, 2, W, 128), F32),
            pltpu.VMEM((4, W, 3 * W), BF),
            pltpu.VMEM((4, 3 * W, W), BF),
            pltpu.VMEM((2 * W, W), BF),
            pltpu.VMEM((2, 2, tiles, edge, 128), F32),
            pltpu.VMEM((2, 2, W, W), F32),
            pltpu.VMEM((2, 2, 3, W + 16, 128), F32),
            pltpu.VMEM((2, 2, 2, W, 128), F32),
            pltpu.VMEM((2, 2, 3 * W, W), BF),
            pltpu.VMEM((2, 2, W, 3 * W), BF),
            pltpu.VMEM((2, W, 2 * W), BF),
            pltpu.VMEM((2, 2, W, W), F32),
            pltpu.VMEM((2, 2, W, W), F32),
            pltpu.VMEM((2, W, W), F32),
            pltpu.SemaphoreType.DMA((12,)),
            pltpu.SemaphoreType.DMA((4,)),
        ],
        compiler_params=pltpu.CompilerParams(vmem_limit_bytes=DATA_VMEM),
        cost_estimate=pl.CostEstimate(flops=COST_FLOPS, bytes_accessed=COST_BYTES, transcendentals=0),
        name="data_terms",
    )(starts, counts, spectrum, pupils, amplitudes, jnp.asarray(packed), jnp.asarray(spread))


def finish_kernel(
    out_in, prow, pcol, ppup, verte_hbm, verto_hbm, sidee_hbm, sideo_hbm, endse_hbm, endso_hbm,
    out_hbm, pup_hbm,
    vert, side, ends, rows_out, cols_out, pup_out, sem_in, sem_out,
):
    edge = out_in.shape[1]
    tiles = edge // 128
    mid = edge - 2 * BAND
    high_row = edge - BAND
    last = 2 * tiles - 1
    ins = {}

    def get(name, src, dst):
        copy = pltpu.make_async_copy(src, dst, sem_in.at[len(ins)])
        copy.start()
        ins[name] = copy

    verts = (verte_hbm, verto_hbm)
    sides = (sidee_hbm, sideo_hbm)
    odd_row, odd_col = parity_of("sy"), parity_of("sx")
    v_at = (1 - odd_row, odd_row)
    s_at = (1 - odd_col, odd_col)
    for c in range(2):
        for i in range(2):
            get(("vert", i, c), verts[i].at[c], vert.at[i, c])
            get(("side", i, c), sides[i].at[c], side.at[i, c])
            get(("ends", i, c), (endse_hbm, endso_hbm)[i].at[c], ends.at[i, c])
    outs = []

    def put(src, dst):
        copy = pltpu.make_async_copy(src, dst, sem_out.at[len(outs)])
        copy.start()
        outs.append(copy)

    def band(t, c, k):
        sub = vert[v_at[t], c, :, pl.ds(k * 128, 128)].astype(F32)
        if k == tiles - 1 or k == tiles:
            sub = sub + vert[v_at[t], c, :, pl.ds((2 * tiles - 1 - k) * 128, 128)].astype(F32)
        if k == 0 or k == last:
            d = 0 if k == 0 else 1
            far = vert[v_at[t], c, :, pl.ds(2 * edge + 4 * W + d * BAND, BAND)].astype(F32)
            sub = sub + (far + ends[s_at[d], c, pl.ds(t * BAND, BAND), :].astype(F32))
        rows_out[t, c, :, pl.ds(k * 128, 128)] = (prow[t, c, k] - 0.5 * sub).astype(BF)

    for c in range(2):
        for i in range(2):
            for name in ("vert", "side", "ends"):
                ins[name, i, c].wait()
        for t in range(2):
            for k in range(last + 1):
                band(t, c, k)
            put(rows_out.at[t, c], out_hbm.at[c, pl.ds(t * high_row, BAND), :])
        for d in range(2):
            sub = side[s_at[d], c, pl.ds(0, mid), :].astype(F32)
            cols_out[d, c] = (pcol[d, c] - 0.5 * sub).astype(BF)
            put(cols_out.at[d, c], out_hbm.at[c, pl.ds(BAND, mid), pl.ds(d * last * 128, 128)])
        for half in range(2):
            rows = pl.ds(half * 128, 128)
            for q in range(4):
                cols = pl.ds(q * 128, 128)
                d = q // 2
                sub = side[s_at[d], c, pl.ds(mid + (q % 2) * W + half * 128, 128), :].astype(F32)
                for t in range(2):
                    sub = sub + vert[v_at[t], c, :, pl.ds(2 * edge + half * 512 + q * 128, 128)].astype(F32)
                pup_out[c, rows, cols] = ppup[c, rows, cols] - 0.5 * sub
        put(pup_out.at[c], pup_hbm.at[c])
    for copy in outs:
        copy.wait()


def finish(out, prow, pcol, ppup, verts, sides, ends):
    edge = out.shape[1]
    tiles = edge // 128
    mid = edge - 2 * BAND
    hbm = pl.BlockSpec(memory_space=pl.ANY)
    vmem = pl.BlockSpec(memory_space=pltpu.VMEM)
    return pl.pallas_call(
        finish_kernel,
        out_shape=(
            jax.ShapeDtypeStruct(out.shape, BF),
            jax.ShapeDtypeStruct(ppup.shape, F32),
        ),
        in_specs=[hbm] + [vmem] * 3 + [hbm] * 6,
        out_specs=(hbm, hbm),
        input_output_aliases={0: 0},
        scratch_shapes=[
            pltpu.VMEM((2,) + verts[0].shape, BF),
            pltpu.VMEM((2,) + sides[0].shape, BF),
            pltpu.VMEM((2,) + ends[0].shape, BF),
            pltpu.VMEM((2, 2, BAND, 2 * edge), BF),
            pltpu.VMEM((2, 2, mid, 128), BF),
            pltpu.VMEM(ppup.shape, F32),
            pltpu.SemaphoreType.DMA((16,)),
            pltpu.SemaphoreType.DMA((10,)),
        ],
        compiler_params=pltpu.CompilerParams(vmem_limit_bytes=FINISH_VMEM),
        cost_estimate=pl.CostEstimate(flops=10_000_000, bytes_accessed=17_000_000, transcendentals=0),
        name="shared_bands",
    )(out, prow, pcol, ppup, *verts, *sides, *ends)


def parity_of(axis):
    return lax.rem(lax.axis_index(axis), 2)


def row_start(flag, edge):
    return pl.ds(pl.multiple_of(flag * (edge - BAND), 128), BAND)


def both_ways(axis):
    odd = parity_of(axis)
    return 1 - odd, odd


def sides_kernel(spec_hbm, pup_hbm, ends_e, ends_o, side_e, side_o, ends_v, side_v, sem_in, sem_out):
    edge, wide = spec_hbm.shape[1], spec_hbm.shape[2]
    mid = edge - 2 * BAND
    right = both_ways("sx")
    ins, outs, plan = [], [], []

    def get(src, dst):
        for c in range(2):
            copy = pltpu.make_async_copy(src.at[c], dst.at[c], sem_in.at[len(ins)])
            copy.start()
            ins.append(copy)

    for i in range(2):
        cols = row_start(right[i], wide)
        for t in range(2):
            get(spec_hbm.at[:, pl.ds(t * (edge - BAND), BAND), cols], ends_v.at[i, :, pl.ds(t * BAND, BAND), :])
        plan.append((len(ins), ends_v.at[i], (ends_e, ends_o)[i]))
    for i in range(2):
        get(spec_hbm.at[:, pl.ds(BAND, mid), row_start(right[i], wide)], side_v.at[i, :, pl.ds(0, mid), :])
        for q in range(2):
            half = pl.ds(pl.multiple_of(right[i] * W + q * 128, 128), 128)
            get(pup_hbm.at[:, :, half], side_v.at[i, :, pl.ds(mid + q * W, W), :])
        plan.append((len(ins), side_v.at[i], (side_e, side_o)[i]))
    send(plan, ins, outs, sem_out)


def send(plan, ins, outs, sem_out):
    done = 0
    for ready, src, dst in plan:
        while done < ready:
            ins[done].wait()
            done += 1
        for c in range(2):
            copy = pltpu.make_async_copy(src.at[c], dst.at[c], sem_out.at[len(outs)])
            copy.start()
            outs.append(copy)
    for copy in outs:
        copy.wait()


def pack_sides(spectrum, pupils):
    edge = spectrum.shape[1]
    hbm = pl.BlockSpec(memory_space=pl.ANY)
    ends = (2, 2 * BAND, BAND)
    side = (2, edge - 2 * BAND + 2 * W, BAND)
    return pl.pallas_call(
        sides_kernel,
        out_shape=tuple(jax.ShapeDtypeStruct(shape, BF) for shape in (ends, ends, side, side)),
        in_specs=[hbm, hbm],
        out_specs=(hbm,) * 4,
        scratch_shapes=[
            pltpu.VMEM((2,) + ends, BF),
            pltpu.VMEM((2,) + side, BF),
            pltpu.SemaphoreType.DMA((20,)),
            pltpu.SemaphoreType.DMA((8,)),
        ],
        compiler_params=pltpu.CompilerParams(vmem_limit_bytes=FULL_VMEM),
        cost_estimate=pl.CostEstimate(flops=1, bytes_accessed=4_000_000, transcendentals=0),
        name="pack_sides",
    )(spectrum, pupils)


def verts_kernel(spec_hbm, pup_hbm, ends_e, ends_o, vert_e, vert_o, vert_v, sem_in, sem_out):
    edge, wide = spec_hbm.shape[1], spec_hbm.shape[2]
    low, right = both_ways("sy"), both_ways("sx")
    ins, outs, plan = [], [], []

    def get(src, dst):
        for c in range(2):
            copy = pltpu.make_async_copy(src.at[c], dst.at[c], sem_in.at[len(ins)])
            copy.start()
            ins.append(copy)

    for i in (1, 0):
        get(spec_hbm.at[:, row_start(low[i], edge), :], vert_v.at[i, :, :, pl.ds(0, wide)])
        for q in range(2):
            get(pup_hbm.at[:, pl.ds(q * 128, 128), :], vert_v.at[i, :, :, pl.ds(wide + q * 2 * W, 2 * W)])
        rows = pl.ds(pl.multiple_of(low[i] * BAND, 128), BAND)
        for j, src in enumerate((ends_e, ends_o)):
            cols = pl.ds(pl.multiple_of(wide + 4 * W + right[j] * BAND, 128), BAND)
            get(src.at[:, rows, :], vert_v.at[i, :, :, cols])
        plan.append((len(ins), vert_v.at[i], (vert_e, vert_o)[i]))
    send(plan, ins, outs, sem_out)


def pack_verts(spectrum, pupils, ends_e, ends_o):
    wide = spectrum.shape[2]
    hbm = pl.BlockSpec(memory_space=pl.ANY)
    vert = (2, BAND, wide + 4 * W + 2 * BAND)
    return pl.pallas_call(
        verts_kernel,
        out_shape=tuple(jax.ShapeDtypeStruct(vert, BF) for _ in range(2)),
        in_specs=[hbm] * 4,
        out_specs=(hbm, hbm),
        scratch_shapes=[
            pltpu.VMEM((2,) + vert, BF),
            pltpu.SemaphoreType.DMA((20,)),
            pltpu.SemaphoreType.DMA((4,)),
        ],
        compiler_params=pltpu.CompilerParams(vmem_limit_bytes=FULL_VMEM),
        cost_estimate=pl.CostEstimate(flops=1, bytes_accessed=8_000_000, transcendentals=0),
        name="pack_verts",
    )(spectrum, pupils, ends_e, ends_o)


def local(spectrum, pupils, amplitudes, crop_starts, led_counts):
    rows = lax.axis_size("sy")
    cols = lax.axis_size("sx")

    def swap(value, axis, count, first):
        pairs = [(i, i + 1) for i in range(first, count - 1, 2)]
        return lax.ppermute(value, axis, pairs + [(j, i) for i, j in pairs])

    ends_e, ends_o, side_e, side_o = pack_sides(spectrum, pupils)
    ends = (swap(ends_e, "sx", cols, 0), swap(ends_o, "sx", cols, 1))
    sides = (swap(side_e, "sx", cols, 0), swap(side_o, "sx", cols, 1))
    vert_e, vert_o = pack_verts(spectrum, pupils, *ends)
    below = swap(vert_o, "sy", rows, 1)
    verts = (swap(vert_e, "sy", rows, 0), below)
    out, prow, pcol, ppup = compute(spectrum, pupils, amplitudes, crop_starts.reshape(-1), led_counts.reshape(-1))
    return finish(out, prow, pcol, ppup, verts, sides, ends)


def solution(mesh):
    placed = (
        P(None, "sy", "sx"),
        P(None, "sy", "sx"),
        P("sy", "sx", None, None, None),
        P("sy", "sx", None, None),
        P("sy", "sx"),
    )
    return jax.shard_map(
        local,
        mesh=mesh,
        in_specs=placed,
        out_specs=(P(None, "sy", "sx"), P(None, "sy", "sx")),
        check_vma=False,
    )
```

```python
import functools
import math

import jax
import jax.numpy as jnp
import ml_dtypes
import numpy as np
from jax import lax
from jax.experimental import pallas as pl
from jax.experimental.pallas import tpu as pltpu
from jax.sharding import PartitionSpec as P

H = 64
MAXL = 4
W = 256
HALF = 128
FLOOR_SQUARE = 0.0625
COST_FLOPS = 20_000_000_000
COST_BYTES = 30_000_000
FULL_VMEM = 60 * 1024 * 1024
VERT_VMEM = 48 * 1024 * 1024
DATA_VMEM = 50 * 1024 * 1024
FINISH_VMEM = 24 * 1024 * 1024
BAND = 2 * H
BF = jnp.bfloat16
F32 = jnp.float32


def halves(table):
    high = table.astype(ml_dtypes.bfloat16)
    low = (table - high.astype(np.float64)).astype(ml_dtypes.bfloat16)
    return high, low


def tables():
    m = np.arange(HALF)[:, None]
    j = np.arange(HALF)[None, :]
    out = []
    for parity in (0, 1):
        phase = ((2 * m + parity) * j % W) * (2.0 * math.pi / W)
        re = np.cos(phase) / math.sqrt(W)
        im = np.sin(phase) / math.sqrt(W)
        left = np.block([[re, -im], [im, re]])
        out.append(left)
        out.append(left.T)
    packed = np.stack([np.stack([halves(t)[part] for t in out]) for part in (0, 1)])
    spread = np.zeros((W, W))
    for p in (0, 1):
        for q in range(HALF):
            spread[2 * q + p, p * HALF + q] = 1.0
    spread = np.concatenate([spread, spread]).astype(ml_dtypes.bfloat16)
    return packed, spread


def split(value):
    high = value.astype(BF)
    low = (value - high.astype(F32)).astype(BF)
    return high, low


def dot(a, b):
    return jnp.dot(a, b, preferred_element_type=F32)


def put_rows(ref, index, rows, cols, value):
    high, low = split(value)
    ref[index, pl.ds(rows, 16), cols] = high
    ref[index, pl.ds(W + rows, 16), cols] = low
    ref[index, pl.ds(2 * W + rows, 16), cols] = high


def put_cols(ref, index, rows, cols, value):
    high, low = split(value)
    ref[index, rows, pl.ds(cols, 128)] = high
    ref[index, rows, pl.ds(W + cols, 128)] = low
    ref[index, rows, pl.ds(2 * W + cols, 128)] = high


def compute_kernel(
    starts, counts, spec_hbm, pup_hbm, amp_hbm, tab_hbm, spread_hbm,
    out_hbm, prow, pcol, ppup,
    spec, pupb, pup, amp, tab_l, tab_r, spread, acc, pacc,
    win, prs, xr, xc, xa, ya, yb, ampq, sem_in, sem_out,
):
    edge = spec.shape[2]
    tiles = edge // 128
    low_row, high_row = BAND, edge - BAND
    mid = high_row - low_row
    copies = []

    def get(src, dst):
        copy = pltpu.make_async_copy(src, dst, sem_in.at[len(copies)])
        copy.start()
        copies.append(copy)

    get(pup_hbm, pupb)
    for h in range(2):
        get(amp_hbm.at[0, :, :, :, pl.ds(h * 128, 128)], amp.at[:, :, h])
    for i, part in enumerate((0, 0, 1)):
        get(tab_hbm.at[part], tab_l.at[:, :, pl.ds(i * W, W)])
        get(tab_hbm.at[part], tab_r.at[:, pl.ds(i * W, W), :])
    get(spread_hbm, spread)
    for g in range(2):
        get(spec_hbm.at[:, :, pl.ds(g * edge, edge)], spec.at[g])

    zero = jnp.zeros((128, 128), F32)

    def clear(i, carry):
        for g in range(2):
            for c in range(2):
                for k in range(tiles):
                    acc[g, c, k, pl.ds(pl.multiple_of(i * 32, 32), 32), :] = zero[:32]
        return carry

    lax.fori_loop(0, edge // 32, clear, 0)
    for c in copies[:-2]:
        c.wait()
    for g in range(2):
        for c in range(2):
            pup[g, c] = pupb[c, :, pl.ds(g * W, W)].astype(F32)
            pacc[g, c] = jnp.zeros((W, W), F32)
    copies[-2].wait()
    copies[-1].wait()
    lane = lax.broadcasted_iota(jnp.int32, (16, 128), 1)

    def slot_stages(g, slot):
        a = starts[0, g, slot, 0]
        b = starts[0, g, slot, 1]
        a0 = pl.multiple_of(jnp.minimum(a // 16 * 16, edge - W - 16), 16)
        off = a - a0
        k0 = jnp.minimum(b // 128, tiles - 3)
        s = b - k0 * 128
        sr = lax.rem(s, 128)
        back_shift = lax.rem(128 - sr, 128)
        from_first = lane >= s
        keep_low = lane < 128 - s
        col0 = pl.multiple_of(k0 * 128, 128)
        for c in range(2):
            for r in range(0, W + 16, 16):
                block = spec[g, c, pl.ds(a0 + r, 16), pl.ds(col0, 384)].astype(F32)
                for i in range(3):
                    win[g, c, i, pl.ds(r, 16), :] = block[:, i * 128 : (i + 1) * 128]
        for c in range(2):
            for r in range(0, W, 16):
                r0 = pltpu.roll(pup[g, c, pl.ds(r, 16), pl.ds(0, 128)], sr, 1)
                r1 = pltpu.roll(pup[g, c, pl.ds(r, 16), pl.ds(128, 128)], sr, 1)
                prs[g, c, 0, pl.ds(r, 16), :] = jnp.where(from_first, r0, r1)
                prs[g, c, 1, pl.ds(r, 16), :] = jnp.where(from_first, r1, r0)

        def crop(c, h, r):
            if h == 1:
                return win[g, c, 1, pl.ds(off + r, 16), :]
            return jnp.where(from_first, win[g, c, 0, pl.ds(off + r, 16), :], win[g, c, 2, pl.ds(off + r, 16), :])

        for p in range(2):
            for h in range(2):
                rows = amp[g, slot, h, pl.ds(p, 128, stride=2), :]
                hi, lo = split(rows)
                xa[g, pl.ds(p * 128, 128), pl.ds(h * 128, 128)] = hi
                xa[g, pl.ds(p * 128, 128), pl.ds(W + h * 128, 128)] = lo
        ampq[g] = dot(xa[g], spread[...])
        yield

        for r in range(0, HALF, 16):
            for h in range(2):
                parts = []
                for rr in (r, r + HALF):
                    cr = crop(0, h, rr)
                    ci = crop(1, h, rr)
                    pr = prs[g, 0, h, pl.ds(rr, 16), :]
                    pi = prs[g, 1, h, pl.ds(rr, 16), :]
                    parts.append((pr * cr - pi * ci, pr * ci + pi * cr))
                for c in range(2):
                    cols = pl.ds(h * 128, 128)
                    put_rows(xr.at[g], 0, c * HALF + r, cols, parts[0][c] + parts[1][c])
                    put_rows(xr.at[g], 1, c * HALF + r, cols, parts[0][c] - parts[1][c])
        for q in range(2):
            ya[g, q] = dot(tab_l[2 * q], xr[g, q])
        yield
        for q in range(2):
            for r in range(0, HALF, 16):
                rows = pl.ds(q * HALF + r, 16)
                for c in range(2):
                    y0 = ya[g, q, pl.ds(c * HALF + r, 16), pl.ds(0, 128)]
                    y1 = ya[g, q, pl.ds(c * HALF + r, 16), pl.ds(128, 128)]
                    put_cols(xc.at[g], 0, rows, c * 128, y0 + y1)
                    put_cols(xc.at[g], 1, rows, c * 128, y0 - y1)
        for u in range(2):
            yb[g, u] = dot(xc[g, u], tab_r[2 * u + 1])
        yield
        for u in range(2):
            for r in range(0, W, 16):
                rows = pl.ds(r, 16)
                re = yb[g, u, rows, pl.ds(0, 128)]
                im = yb[g, u, rows, pl.ds(128, 128)]
                power = jnp.maximum(re * re + im * im, FLOOR_SQUARE)
                keeper = 1.0 - ampq[g, rows, pl.ds(u * 128, 128)] * lax.rsqrt(power)
                put_cols(xc.at[g], u, rows, 0, re * keeper)
                put_cols(xc.at[g], u, rows, 128, im * keeper)
        for u in range(2):
            ya[g, u] = dot(xc[g, u], tab_r[2 * u])
        yield
        for q in range(2):
            for r in range(0, HALF, 16):
                rows = pl.ds(q * HALF + r, 16)
                for c in range(2):
                    e = ya[g, 0, rows, pl.ds(c * 128, 128)]
                    o = ya[g, 1, rows, pl.ds(c * 128, 128)]
                    put_rows(xr.at[g], q, c * HALF + r, pl.ds(0, 128), e + o)
                    put_rows(xr.at[g], q, c * HALF + r, pl.ds(128, 128), e - o)
        for q in range(2):
            yb[g, q] = dot(tab_l[2 * q + 1], xr[g, q])
        yield
        for r in range(0, HALF, 16):
            for rr in (r, r + HALF):
                rows = pl.ds(a + rr, 16)
                old = [[acc[g, c, k0 + i, rows, :] for i in range(3)] for c in range(2)]
                drop, terms = [], []
                for h in range(2):
                    back = []
                    for c in range(2):
                        e = yb[g, 0, pl.ds(c * HALF + r, 16), pl.ds(h * 128, 128)]
                        o = yb[g, 1, pl.ds(c * HALF + r, 16), pl.ds(h * 128, 128)]
                        back.append(e + o if rr == r else e - o)
                    br, bi = back
                    pr = prs[g, 0, h, pl.ds(rr, 16), :]
                    pi = prs[g, 1, h, pl.ds(rr, 16), :]
                    cr = crop(0, h, rr)
                    ci = crop(1, h, rr)
                    drop.append((pr * br + pi * bi, pr * bi - pi * br))
                    terms.append((cr * br + ci * bi, cr * bi - ci * br))
                for c in range(2):
                    acc[g, c, k0, rows, :] = old[c][0] + jnp.where(from_first, drop[0][c], 0.0)
                    acc[g, c, k0 + 1, rows, :] = old[c][1] + drop[1][c]
                    acc[g, c, k0 + 2, rows, :] = old[c][2] + jnp.where(from_first, 0.0, drop[0][c])
                for c in range(2):
                    t0 = pltpu.roll(terms[0][c], back_shift, 1)
                    t1 = pltpu.roll(terms[1][c], back_shift, 1)
                    pacc[g, c, pl.ds(rr, 16), pl.ds(0, 128)] += jnp.where(keep_low, t0, t1)
                    pacc[g, c, pl.ds(rr, 16), pl.ds(128, 128)] += jnp.where(keep_low, t1, t0)

    def weight(inside):
        return jnp.where(inside, F32(1.0), F32(0.0))

    row, col = lax.axis_index("sy"), lax.axis_index("sx")
    up, down = weight(row > 0), weight(row < lax.axis_size("sy") - 1)
    left_out, right_out = weight(col > 0), weight(col < lax.axis_size("sx") - 1)
    pending = []

    def put(src, dst):
        copy = pltpu.make_async_copy(src, dst, sem_out.at[len(pending)])
        copy.start()
        pending.append(copy)

    def run(segments):
        def step(slot, carry):
            stages = [slot_stages(g, slot) for g in segments]
            while stages:
                stages = [stage for stage in stages if next(stage, stage) is not stage]
            return carry

        return step

    both = jnp.minimum(counts[0, 0], counts[0, 1])
    lax.fori_loop(0, both, run((0, 1)), 0)
    for g in range(2):
        lax.fori_loop(both, counts[0, g], run((g,)), 0)
    for c in range(2):

        def finish(i, carry, c=c):
            rows = pl.ds(pl.multiple_of(low_row + i * 64, 64), 64)
            for k in range(1, tiles - 1):
                for g in range(2):
                    spec[g, c, rows, pl.ds(k * 128, 128)] = acc[g, c, k, rows, :].astype(BF)
            end = pl.ds((tiles - 1) * 128, 128)
            start = pl.ds(0, 128)
            gap = 0.5 * (spec[0, c, rows, end].astype(F32) - spec[1, c, rows, start].astype(F32))
            spec[0, c, rows, end] = (acc[0, c, tiles - 1, rows, :] + gap).astype(BF)
            spec[1, c, rows, start] = (acc[1, c, 0, rows, :] - gap).astype(BF)
            return carry

        lax.fori_loop(0, mid // 64, finish, 0)
        for g in range(2):
            first_tile = 1 - g
            cols = (tiles - 1) * 128
            put(
                spec.at[g, c, pl.ds(low_row, mid), pl.ds(first_tile * 128, cols)],
                out_hbm.at[c, pl.ds(low_row, mid), pl.ds((g * tiles + first_tile) * 128, cols)],
            )
    for g in range(2):
        left = left_out if g == 0 else F32(1.0)
        right = right_out if g == 1 else F32(1.0)
        neighbours = up + down + left + right
        for c in range(2):
            ppup[c, :, pl.ds(g * W, W)] = pacc[g, c] + 0.5 * (neighbours * pup[g, c] - pup[1 - g, c])
        for c in range(2):
            for k in range(tiles):
                side = left if k == 0 else right if k == tiles - 1 else None
                local = (k == 0 and g == 1) or (k == tiles - 1 and g == 0)
                for t, (first, vert) in enumerate(((0, up), (high_row, down))):
                    factor = vert if side is None else (1.0 + vert) * (1.0 + side) - 1.0
                    own = spec[g, c, pl.ds(first, BAND), pl.ds(k * 128, 128)].astype(F32)
                    add = (0.5 * factor) * own
                    if local:
                        other = spec[1 - g, c, pl.ds(first, BAND), pl.ds((tiles - 1 - k) * 128, 128)].astype(F32)
                        add = add - 0.5 * other
                    prow[t, c, g * tiles + k] = acc[g, c, k, pl.ds(first, BAND), :] + add
        k_out = 0 if g == 0 else tiles - 1
        w_out = left_out if g == 0 else right_out
        for c in range(2):

            def outer(i, carry, c=c):
                rows = pl.ds(pl.multiple_of(low_row + i * 128, 128), 128)
                add = (0.5 * w_out) * spec[g, c, rows, pl.ds(k_out * 128, 128)].astype(F32)
                pcol[g, c, pl.ds(pl.multiple_of(i * 128, 128), 128), :] = acc[g, c, k_out, rows, :] + add
                return carry

            lax.fori_loop(0, mid // 128, outer, 0)
    for copy in pending:
        copy.wait()


def compute(spectrum, pupils, amplitudes, starts, counts):
    edge = spectrum.shape[1]
    tiles = edge // 128
    mid = edge - 2 * BAND
    packed, spread = tables()
    hbm = pl.BlockSpec(memory_space=pl.ANY)
    smem = pl.BlockSpec(memory_space=pltpu.SMEM)
    vmem = pl.BlockSpec(memory_space=pltpu.VMEM)
    return pl.pallas_call(
        compute_kernel,
        out_shape=(
            jax.ShapeDtypeStruct(spectrum.shape, BF),
            pltpu.VMEM((2, 2, 2 * tiles, BAND, 128), F32),
            pltpu.VMEM((2, 2, mid, 128), F32),
            pltpu.VMEM(pupils.shape, F32),
        ),
        in_specs=[smem, smem] + [hbm] * 5,
        out_specs=(hbm, vmem, vmem, vmem),
        scratch_shapes=[
            pltpu.VMEM((2, 2, edge, edge), BF),
            pltpu.VMEM((2, W, 2 * W), BF),
            pltpu.VMEM((2, 2, W, W), F32),
            pltpu.VMEM((2, MAXL, 2, W, 128), F32),
            pltpu.VMEM((4, W, 3 * W), BF),
            pltpu.VMEM((4, 3 * W, W), BF),
            pltpu.VMEM((2 * W, W), BF),
            pltpu.VMEM((2, 2, tiles, edge, 128), F32),
            pltpu.VMEM((2, 2, W, W), F32),
            pltpu.VMEM((2, 2, 3, W + 16, 128), F32),
            pltpu.VMEM((2, 2, 2, W, 128), F32),
            pltpu.VMEM((2, 2, 3 * W, W), BF),
            pltpu.VMEM((2, 2, W, 3 * W), BF),
            pltpu.VMEM((2, W, 2 * W), BF),
            pltpu.VMEM((2, 2, W, W), F32),
            pltpu.VMEM((2, 2, W, W), F32),
            pltpu.VMEM((2, W, W), F32),
            pltpu.SemaphoreType.DMA((12,)),
            pltpu.SemaphoreType.DMA((4,)),
        ],
        compiler_params=pltpu.CompilerParams(vmem_limit_bytes=DATA_VMEM),
        cost_estimate=pl.CostEstimate(flops=COST_FLOPS, bytes_accessed=COST_BYTES, transcendentals=0),
        name="data_terms",
    )(starts, counts, spectrum, pupils, amplitudes, jnp.asarray(packed), jnp.asarray(spread))


def finish_kernel(
    out_in, prow, pcol, ppup, verto_hbm, verte_hbm, sidee_hbm, sideo_hbm, endse_hbm, endso_hbm,
    out_hbm, pup_hbm,
    vert, side, ends, rows_out, cols_out, pup_out, sem_in, sem_out,
):
    edge = out_in.shape[1]
    tiles = edge // 128
    mid = edge - 2 * BAND
    high_row = edge - BAND
    last = 2 * tiles - 1
    ins = {}

    def get(name, src, dst):
        copy = pltpu.make_async_copy(src, dst, sem_in.at[len(ins)])
        copy.start()
        ins[name] = copy

    verts = (verte_hbm, verto_hbm)
    sides = (sidee_hbm, sideo_hbm)
    odd_row, odd_col = parity_of("sy"), parity_of("sx")
    v_at = (1 - odd_row, odd_row)
    s_at = (1 - odd_col, odd_col)
    for c in range(2):
        for i in range(2):
            get(("vert", i, c), verts[i].at[c], vert.at[i, c])
            get(("side", i, c), sides[i].at[c], side.at[i, c])
            get(("ends", i, c), (endse_hbm, endso_hbm)[i].at[c], ends.at[i, c])
    outs = []

    def put(src, dst):
        copy = pltpu.make_async_copy(src, dst, sem_out.at[len(outs)])
        copy.start()
        outs.append(copy)

    def band(t, c, k):
        sub = vert[v_at[t], c, :, pl.ds(k * 128, 128)].astype(F32)
        if k == tiles - 1 or k == tiles:
            sub = sub + vert[v_at[t], c, :, pl.ds((2 * tiles - 1 - k) * 128, 128)].astype(F32)
        if k == 0 or k == last:
            d = 0 if k == 0 else 1
            far = vert[v_at[t], c, :, pl.ds(2 * edge + 4 * W + d * BAND, BAND)].astype(F32)
            sub = sub + (far + ends[s_at[d], c, pl.ds(t * BAND, BAND), :].astype(F32))
        rows_out[t, c, :, pl.ds(k * 128, 128)] = (prow[t, c, k] - 0.5 * sub).astype(BF)

    for c in range(2):
        for i in range(2):
            for name in ("vert", "side", "ends"):
                ins[name, i, c].wait()
        for t in range(2):
            for k in range(last + 1):
                band(t, c, k)
            put(rows_out.at[t, c], out_hbm.at[c, pl.ds(t * high_row, BAND), :])
        for d in range(2):
            sub = side[s_at[d], c, pl.ds(0, mid), :].astype(F32)
            cols_out[d, c] = (pcol[d, c] - 0.5 * sub).astype(BF)
            put(cols_out.at[d, c], out_hbm.at[c, pl.ds(BAND, mid), pl.ds(d * last * 128, 128)])
        for half in range(2):
            rows = pl.ds(half * 128, 128)
            for q in range(4):
                cols = pl.ds(q * 128, 128)
                d = q // 2
                sub = side[s_at[d], c, pl.ds(mid + (q % 2) * W + half * 128, 128), :].astype(F32)
                for t in range(2):
                    sub = sub + vert[v_at[t], c, :, pl.ds(2 * edge + half * 512 + q * 128, 128)].astype(F32)
                pup_out[c, rows, cols] = ppup[c, rows, cols] - 0.5 * sub
        put(pup_out.at[c], pup_hbm.at[c])
    for copy in outs:
        copy.wait()


def finish(out, prow, pcol, ppup, verts, sides, ends):
    edge = out.shape[1]
    tiles = edge // 128
    mid = edge - 2 * BAND
    hbm = pl.BlockSpec(memory_space=pl.ANY)
    vmem = pl.BlockSpec(memory_space=pltpu.VMEM)
    return pl.pallas_call(
        finish_kernel,
        out_shape=(
            jax.ShapeDtypeStruct(out.shape, BF),
            jax.ShapeDtypeStruct(ppup.shape, F32),
        ),
        in_specs=[hbm] + [vmem] * 3 + [hbm] * 6,
        out_specs=(hbm, hbm),
        input_output_aliases={0: 0},
        scratch_shapes=[
            pltpu.VMEM((2,) + verts[0].shape, BF),
            pltpu.VMEM((2,) + sides[0].shape, BF),
            pltpu.VMEM((2,) + ends[0].shape, BF),
            pltpu.VMEM((2, 2, BAND, 2 * edge), BF),
            pltpu.VMEM((2, 2, mid, 128), BF),
            pltpu.VMEM(ppup.shape, F32),
            pltpu.SemaphoreType.DMA((16,)),
            pltpu.SemaphoreType.DMA((10,)),
        ],
        compiler_params=pltpu.CompilerParams(vmem_limit_bytes=FINISH_VMEM),
        cost_estimate=pl.CostEstimate(flops=10_000_000, bytes_accessed=17_000_000, transcendentals=0),
        name="shared_bands",
    )(out, prow, pcol, ppup, verts[1], verts[0], *sides, *ends)


def parity_of(axis):
    return lax.rem(lax.axis_index(axis), 2)


def row_start(flag, edge):
    return pl.ds(pl.multiple_of(flag * (edge - BAND), 128), BAND)


def both_ways(axis):
    odd = parity_of(axis)
    return 1 - odd, odd


def sides_kernel(spec_hbm, pup_hbm, ends_e, ends_o, side_e, side_o, ends_v, side_v, sem_in, sem_out):
    edge, wide = spec_hbm.shape[1], spec_hbm.shape[2]
    mid = edge - 2 * BAND
    right = both_ways("sx")
    ins, outs, plan = [], [], []

    def get(src, dst):
        for c in range(2):
            copy = pltpu.make_async_copy(src.at[c], dst.at[c], sem_in.at[len(ins)])
            copy.start()
            ins.append(copy)

    for i in range(2):
        cols = row_start(right[i], wide)
        for t in range(2):
            get(spec_hbm.at[:, pl.ds(t * (edge - BAND), BAND), cols], ends_v.at[i, :, pl.ds(t * BAND, BAND), :])
        plan.append((len(ins), ends_v.at[i], (ends_e, ends_o)[i]))
    for i in range(2):
        get(spec_hbm.at[:, pl.ds(BAND, mid), row_start(right[i], wide)], side_v.at[i, :, pl.ds(0, mid), :])
        for q in range(2):
            half = pl.ds(pl.multiple_of(right[i] * W + q * 128, 128), 128)
            get(pup_hbm.at[:, :, half], side_v.at[i, :, pl.ds(mid + q * W, W), :])
        plan.append((len(ins), side_v.at[i], (side_e, side_o)[i]))
    send(plan, ins, outs, sem_out)


def send(plan, ins, outs, sem_out):
    done = 0
    for ready, src, dst in plan:
        while done < ready:
            ins[done].wait()
            done += 1
        for c in range(2):
            copy = pltpu.make_async_copy(src.at[c], dst.at[c], sem_out.at[len(outs)])
            copy.start()
            outs.append(copy)
    for copy in outs:
        copy.wait()


def pack_sides(spectrum, pupils):
    edge = spectrum.shape[1]
    hbm = pl.BlockSpec(memory_space=pl.ANY)
    ends = (2, 2 * BAND, BAND)
    side = (2, edge - 2 * BAND + 2 * W, BAND)
    return pl.pallas_call(
        sides_kernel,
        out_shape=tuple(jax.ShapeDtypeStruct(shape, BF) for shape in (ends, ends, side, side)),
        in_specs=[hbm, hbm],
        out_specs=(hbm,) * 4,
        scratch_shapes=[
            pltpu.VMEM((2,) + ends, BF),
            pltpu.VMEM((2,) + side, BF),
            pltpu.SemaphoreType.DMA((20,)),
            pltpu.SemaphoreType.DMA((8,)),
        ],
        compiler_params=pltpu.CompilerParams(vmem_limit_bytes=FULL_VMEM),
        cost_estimate=pl.CostEstimate(flops=1, bytes_accessed=4_000_000, transcendentals=0),
        name="pack_sides",
    )(spectrum, pupils)


def vert_kernel(odd_pairs, spec_hbm, pup_hbm, ends_e, ends_o, vert, vert_v, sem_in, sem_out):
    edge, wide = spec_hbm.shape[1], spec_hbm.shape[2]
    low, right = both_ways("sy")[odd_pairs], both_ways("sx")
    ins, outs = [], []

    def get(src, dst):
        for c in range(2):
            copy = pltpu.make_async_copy(src.at[c], dst.at[c], sem_in.at[len(ins)])
            copy.start()
            ins.append(copy)

    get(spec_hbm.at[:, row_start(low, edge), :], vert_v.at[:, :, pl.ds(0, wide)])
    for q in range(2):
        get(pup_hbm.at[:, pl.ds(q * 128, 128), :], vert_v.at[:, :, pl.ds(wide + q * 2 * W, 2 * W)])
    rows = pl.ds(pl.multiple_of(low * BAND, 128), BAND)
    for j, src in enumerate((ends_e, ends_o)):
        cols = pl.ds(pl.multiple_of(wide + 4 * W + right[j] * BAND, 128), BAND)
        get(src.at[:, rows, :], vert_v.at[:, :, cols])
    send([(len(ins), vert_v, vert)], ins, outs, sem_out)


def pack_vert(odd_pairs, spectrum, pupils, ends_e, ends_o):
    wide = spectrum.shape[2]
    hbm = pl.BlockSpec(memory_space=pl.ANY)
    vert = (2, BAND, wide + 4 * W + 2 * BAND)
    return pl.pallas_call(
        functools.partial(vert_kernel, odd_pairs),
        out_shape=jax.ShapeDtypeStruct(vert, BF),
        in_specs=[hbm] * 4,
        out_specs=hbm,
        scratch_shapes=[
            pltpu.VMEM(vert, BF),
            pltpu.SemaphoreType.DMA((10,)),
            pltpu.SemaphoreType.DMA((2,)),
        ],
        compiler_params=pltpu.CompilerParams(vmem_limit_bytes=VERT_VMEM),
        cost_estimate=pl.CostEstimate(flops=1, bytes_accessed=4_000_000, transcendentals=0),
        name="pack_odd" if odd_pairs else "pack_even",
    )(spectrum, pupils, ends_e, ends_o)


def local(spectrum, pupils, amplitudes, crop_starts, led_counts):
    rows = lax.axis_size("sy")
    cols = lax.axis_size("sx")

    def swap(value, axis, count, first):
        pairs = [(i, i + 1) for i in range(first, count - 1, 2)]
        return lax.ppermute(value, axis, pairs + [(j, i) for i, j in pairs])

    ends_e, ends_o, side_e, side_o = pack_sides(spectrum, pupils)
    ends = (swap(ends_e, "sx", cols, 0), swap(ends_o, "sx", cols, 1))
    sides = (swap(side_e, "sx", cols, 0), swap(side_o, "sx", cols, 1))
    odd = swap(pack_vert(1, spectrum, pupils, *ends), "sy", rows, 1)
    verts = (swap(pack_vert(0, spectrum, pupils, *ends), "sy", rows, 0), odd)
    out, prow, pcol, ppup = compute(spectrum, pupils, amplitudes, crop_starts, led_counts)
    return finish(out, prow, pcol, ppup, verts, sides, ends)


def solution(mesh):
    placed = (
        P(None, "sy", "sx"),
        P(None, "sy", "sx"),
        P("sy", "sx", None, None, None),
        P("sy", "sx", None, None),
        P("sy", "sx"),
    )
    return jax.shard_map(
        local,
        mesh=mesh,
        in_specs=placed,
        out_specs=(P(None, "sy", "sx"), P(None, "sy", "sx")),
        check_vma=False,
    )
```
